32 devices in a mesh: grp: 2 (over y), vec: 4 (over z), occ: 2 (over x), wlk: 2 (over core).
Axes of the slice: x: 2, y: 2, z: 4, core: 2. Of those that a mesh axis runs over, the one named last changes fastest.
Arguments:
- chol_half: bfloat16 [256, 256, 2048], P(('grp', 'vec'), 'occ'), parts along dimension 0, may hold values from -0.046875 to 0.046875
- theta: bfloat16 [8, 2048, 256], P(('grp', 'wlk'), 'vec', 'occ'), parts along dimension 0, may hold values from -6 to 6
Outputs:
- theta_grad: float32 [8, 2048, 256], P(('grp', 'wlk'), 'vec', 'occ'), parts along dimension 0
The draws below stay inside these ranges and needn't reach their ends.
There are 2 independent parts, one for each index of `grp`. The reference program is written for one: setup_inputs(seed, part) draws one part's arguments, and reference() takes and returns one part's arrays. A program takes and returns all parts, laid end to end along the dimension named above; each array names one. Nothing has to cross between parts.
All inputs are finite; a program needn't handle non-finite values.
Results may differ from the reference program's by a relative error of at most 0.0042.
Values may be sent and summed in bfloat16 or wider, within the bound.
No kernel may reach another device: no remote copies, remote signals or barrier semaphores. Data moves between devices by JAX's collectives and lax.ppermute only.
A program may use at most 64 MiB of HBM per device.

```python
import jax
import jax.numpy as jnp
from jax import lax

M = 2048
O = 256
NCHOL = 128
W = 4


def steps_of(own_key, shape, cuts, least, largest):
    loudness, own = 1.0, jax.random.fold_in(own_key, 6)
    for axis_at, shards_of in cuts:
        steps = jnp.exp(jax.random.uniform(jax.random.fold_in(own, axis_at), (shards_of,), jnp.float32, least / len(cuts), largest / len(cuts)))
        loudness = loudness * jnp.repeat(steps, shape[axis_at] // shards_of).reshape([-1 if axis == axis_at else 1 for axis in range(len(shape))])
    return loudness


def scatter_about(rng, shape, scale, reach, shards=(), kind=jnp.bfloat16):
    loudness = steps_of(rng, shape, shards, -0.22, 0.18) if shards else 1.0
    drawn = jax.random.normal(rng, shape, jnp.float32) * scale * loudness
    return jnp.minimum(jnp.maximum(drawn, -reach), reach).astype(kind)


def setup_inputs(seed: int = 0, part: int = 0) -> dict:
    key_list = jax.random.split(jax.random.key(seed), 3)
    own_keys = jax.random.split(jax.random.fold_in(key_list[2], part), 3)
    return {
        "chol_half": scatter_about(own_keys[0], (NCHOL, O, M), (7 * M) ** -0.5, 0.046875, ((0, 4), (1, 2))),
        "theta": scatter_about(own_keys[1], (W, M, O), 1.0, 6.0, ((0, 2), (1, 4), (2, 2))),
    }


def reference(chol_half, theta):
    walkers = theta.shape[0]

    def add_vector(carry, factor):
        grads = []
        for walker in range(walkers):
            amplitudes = jnp.dot(factor, theta[walker], preferred_element_type=jnp.float32).astype(jnp.bfloat16)
            grads.append(jnp.dot(factor.T, amplitudes.T, preferred_element_type=jnp.float32))
        return carry + jnp.stack(grads), None

    initial = jnp.zeros((walkers, M, O), jnp.float32)
    total, unused = lax.scan(add_vector, initial, chol_half)
    return -total
```

```python
import functools

import jax
import jax.numpy as jnp
from jax import lax
from jax.experimental import pallas as pl
from jax.experimental.pallas import tpu as pltpu
from jax.sharding import PartitionSpec as P

AXES = ("grp", "vec", "occ", "wlk")


def general(chol_half, theta):
    widened = lax.all_gather(theta, "occ", axis=2, tiled=True)
    amplitude_sums = jnp.einsum(
        "gip,wpj->wgij",
        chol_half,
        lax.all_gather(widened, "vec", axis=1, tiled=True),
        preferred_element_type=jnp.float32,
    )
    amplitudes = amplitude_sums.astype(jnp.bfloat16)
    swapped = lax.all_to_all(amplitudes, "occ", split_axis=3, concat_axis=2, tiled=True)
    summed_rows = lax.psum_scatter(
        jnp.einsum("gap,wgba->pwb", chol_half, swapped, preferred_element_type=jnp.float32),
        "vec",
        scatter_dimension=0,
        tiled=True,
    )
    owned = lax.psum_scatter(summed_rows, "occ", scatter_dimension=2, tiled=True)
    return -jnp.transpose(owned, (1, 0, 2))


def amplitude_body(shards, sides, place, factors, *refs):
    pieces, outs, rows = refs[: shards * sides], refs[shards * sides : -1], refs[-1]
    owned, width = pieces[0].shape

    @pl.when(pl.program_id(0) == 0)
    def gather():
        for side in range(sides):
            for step in range(shards):
                at = lax.rem(place[0] + shards - step, shards)
                rows[pl.ds(pl.multiple_of(at * owned, owned), owned), side * width : (side + 1) * width] = pieces[side * shards + step][...]

    sums = jnp.dot(factors[...], rows[...], preferred_element_type=jnp.float32).astype(jnp.bfloat16)
    for side in range(sides):
        outs[side][...] = sums[:, side * width : (side + 1) * width]


def amplitudes_of(place, factors, sides, first, count, block):
    shards, (owned, width) = len(sides[0]), sides[0][0].shape
    orbitals = factors.shape[1]
    return pl.pallas_call(
        functools.partial(amplitude_body, shards, len(sides)),
        grid_spec=pltpu.PrefetchScalarGridSpec(
            num_scalar_prefetch=1,
            grid=(count // block,),
            in_specs=[pl.BlockSpec((block, orbitals), lambda i, place: (i + first // block, 0))]
            + [pl.BlockSpec((owned, width), lambda i, place: (0, 0))] * (shards * len(sides)),
            out_specs=[pl.BlockSpec((block, width), lambda i, place: (i, 0))] * len(sides),
            scratch_shapes=[pltpu.VMEM((orbitals, width * len(sides)), jnp.bfloat16)],
        ),
        out_shape=[jax.ShapeDtypeStruct((count, width), jnp.bfloat16)] * len(sides),
        cost_estimate=pl.CostEstimate(
            flops=2 * count * orbitals * width * len(sides), transcendentals=0, bytes_accessed=2 * count * orbitals
        ),
    )(place, factors, *[piece for side in sides for piece in side])


def gradient_body(shards, starts, place, factors, *refs):
    counts = [len(side) - 1 for side in starts]
    parts, outs, sums = refs[: sum(counts)], refs[sum(counts) : -1], refs[-1]
    step, width = pl.program_id(0), parts[0].shape[1]

    @pl.when(step == 0)
    def clear():
        sums[...] = jnp.zeros_like(sums)

    at = 0
    for side, cuts in enumerate(starts):
        for part, (low, high) in enumerate(zip(cuts[:-1], cuts[1:])):

            @pl.when((step >= low) & (step < high))
            def add(side=side, ref=parts[at + part]):
                vectors = ref.shape[0] // width
                wide = jnp.concatenate([ref[g * width : (g + 1) * width, :] for g in range(vectors)], axis=1)
                sums[side * width : (side + 1) * width, :] += jnp.dot(wide, factors[...], preferred_element_type=jnp.float32)

        at += counts[side]

    @pl.when(step == pl.num_programs(0) - 1)
    def finish():
        owned = sums.shape[1] // shards
        for side in range(len(starts)):
            for hop in range(shards):
                target = lax.rem(place[0] + hop, shards)
                out = outs[side * shards + hop]
                out[...] = sums[side * width : (side + 1) * width, pl.ds(pl.multiple_of(target * owned, owned), owned)].astype(out.dtype)


def gradients_of(place, factors, sides, block, shards, kinds):
    count, orbitals = factors.shape
    width = sides[0][0].shape[1]
    starts, specs, flat = [], [], []
    for side in sides:
        cuts = [0]
        for chunk in side:
            low, steps = cuts[-1], chunk.shape[0] // block
            specs.append(pl.BlockSpec((block, width), lambda i, place, low=low, steps=steps: (jnp.clip(i - low, 0, steps - 1), 0)))
            cuts.append(low + steps)
            flat.append(chunk)
        starts.append(tuple(cuts))
    owned = orbitals // shards
    outs = [kind if hop == 0 else jnp.bfloat16 for kind in kinds for hop in range(shards)]
    got = pl.pallas_call(
        functools.partial(gradient_body, shards, tuple(starts)),
        grid_spec=pltpu.PrefetchScalarGridSpec(
            num_scalar_prefetch=1,
            grid=(count // block,),
            in_specs=[pl.BlockSpec((block, orbitals), lambda i, place: (i, 0))] + specs,
            out_specs=[pl.BlockSpec((width, owned), lambda i, place: (0, 0))] * len(outs),
            scratch_shapes=[pltpu.VMEM((width * len(sides), orbitals), jnp.float32)],
        ),
        out_shape=[jax.ShapeDtypeStruct((width, owned), kind) for kind in outs],
        cost_estimate=pl.CostEstimate(
            flops=2 * count * orbitals * width * len(sides), transcendentals=0, bytes_accessed=2 * count * orbitals
        ),
    )(place, factors, *flat)
    return [got[side * shards : (side + 1) * shards] for side in range(len(sides))]


def total_body(walkers, *refs):
    out, each = refs[-1], (len(refs) - 1) // walkers
    for walker in range(walkers):
        total = refs[walker * each][...].astype(jnp.float32)
        for part in refs[walker * each + 1 : (walker + 1) * each]:
            total = total + part[...].astype(jnp.float32)
        out[walker] = -total.T


def totals_of(pieces):
    width, owned = pieces[0][0].shape
    return pl.pallas_call(
        functools.partial(total_body, len(pieces)),
        out_shape=jax.ShapeDtypeStruct((len(pieces), owned, width), jnp.float32),
    )(*[piece for walker in pieces for piece in walker])


def paired(shape, chol_half, theta):
    shards = shape["vec"]
    vectors, width, orbitals = chol_half.shape
    walkers = theta.shape[0]
    factors = chol_half.reshape(vectors * width, orbitals)
    place = lax.axis_index("vec").reshape(1)

    def flat(grp, vec, occ, wlk):
        return ((grp * shape["vec"] + vec) * shape["occ"] + occ) * shape["wlk"] + wlk

    def moved(value, hop, across):
        pairs = [
            (flat(grp, vec, occ, wlk), flat(grp, (vec + hop) % shards, 1 - occ if across else occ, wlk))
            for grp in range(shape["grp"])
            for vec in range(shards)
            for occ in range(shape["occ"])
            for wlk in range(shape["wlk"])
        ]
        return lax.ppermute(value, AXES, pairs)

    owns, others = [], []
    for walker in range(walkers):
        mine = theta[walker]
        others.append([moved(mine, hop, True) for hop in range(shards)])
        owns.append([mine] + [moved(mine, hop, False) for hop in range(1, shards)])

    block = 4 * width
    cuts = [(0, vectors // 4, vectors), (0, vectors // 2, vectors)]
    kept, received = [], []
    for walker in range(walkers):
        bounds = cuts[min(walker, 1)]
        got = []
        for low, high in zip(bounds[:-1], bounds[1:]):
            (sent,) = amplitudes_of(place, factors, [others[walker]], low * width, (high - low) * width, block)
            got.append(moved(sent, 0, True))
        received.append(got)
        kept.append(amplitudes_of(place, factors, [owns[walker]], 0, vectors * width, block))

    pieces = []
    for walker in range(walkers):
        (own,) = gradients_of(place, factors, [kept[walker]], 2 * block, shards, [jnp.float32])
        (far,) = gradients_of(place, factors, [received[walker]], 2 * block, shards, [jnp.bfloat16])
        pieces.append(
            [own[0]]
            + [moved(own[hop], hop, False) for hop in range(1, shards)]
            + [moved(far[hop], hop, True) for hop in range(shards)]
        )
    return totals_of(pieces)


def solution(mesh):
    placed = (P(("grp", "vec"), "occ", None), P(("grp", "wlk"), "vec", "occ"))
    on_device = functools.partial(paired, dict(mesh.shape)) if mesh.shape["occ"] == 2 else general
    return jax.shard_map(
        on_device,
        mesh=mesh,
        in_specs=placed,
        out_specs=P(("grp", "wlk"), "vec", "occ"),
        check_vma=False,
    )
```

```python
import functools

import jax
import jax.numpy as jnp
from jax import lax
from jax.experimental import pallas as pl
from jax.experimental.pallas import tpu as pltpu
from jax.sharding import PartitionSpec as P

AXES = ("grp", "vec", "occ", "wlk")
SMALL = pltpu.CompilerParams(vmem_limit_bytes=24 * 2**20)


def general(chol_half, theta):
    widened = lax.all_gather(theta, "occ", axis=2, tiled=True)
    amplitude_sums = jnp.einsum(
        "gip,wpj->wgij",
        chol_half,
        lax.all_gather(widened, "vec", axis=1, tiled=True),
        preferred_element_type=jnp.float32,
    )
    amplitudes = amplitude_sums.astype(jnp.bfloat16)
    swapped = lax.all_to_all(amplitudes, "occ", split_axis=3, concat_axis=2, tiled=True)
    summed_rows = lax.psum_scatter(
        jnp.einsum("gap,wgba->pwb", chol_half, swapped, preferred_element_type=jnp.float32),
        "vec",
        scatter_dimension=0,
        tiled=True,
    )
    owned = lax.psum_scatter(summed_rows, "occ", scatter_dimension=2, tiled=True)
    return -jnp.transpose(owned, (1, 0, 2))


def amplitude_body(shards, first, block, place, factors, *refs):
    pieces, own, far, rows = refs[:-3], refs[-3], refs[-2], refs[-1]
    owned, width = pieces[0].shape[0], own.shape[1]
    for step in range(shards):
        at = pl.multiple_of(lax.rem(place[0] + shards - step, shards) * owned, owned)
        if len(pieces) == shards:
            rows[pl.ds(at, owned), :] = pieces[step][...]
        else:
            rows[pl.ds(at, owned), :width] = pieces[step][...]
            rows[pl.ds(at, owned), width:] = pieces[shards + step][...]
    for low in range(0, own.shape[0], block):
        high = min(low + block, own.shape[0])
        sums = jnp.dot(factors[first + low : first + high, :], rows[...], preferred_element_type=jnp.float32).astype(jnp.bfloat16)
        own[low:high, :] = sums[:, :width]
        far[low:high, :] = sums[:, width:]


def amplitudes_of(place, factors, pieces, first, count, width, block=1024):
    shards, orbitals = factors.shape[1] // pieces[0].shape[0], factors.shape[1]
    return pl.pallas_call(
        functools.partial(amplitude_body, shards, first, block),
        in_specs=[pl.BlockSpec(memory_space=pltpu.SMEM)] + [pl.BlockSpec(memory_space=pltpu.VMEM)] * (1 + len(pieces)),
        out_specs=[pl.BlockSpec(memory_space=pltpu.VMEM)] * 2,
        scratch_shapes=[pltpu.VMEM((orbitals, 2 * width), jnp.bfloat16)],
        out_shape=[jax.ShapeDtypeStruct((count, width), jnp.bfloat16)] * 2,
        compiler_params=SMALL,
        cost_estimate=pl.CostEstimate(flops=4 * count * orbitals * width, transcendentals=0, bytes_accessed=2 * count * orbitals),
    )(place, factors, *pieces)


def gradient_body(shards, counts, block, joined, place, factors, *refs):
    parts, outs, sums = refs[: sum(counts)], refs[sum(counts) : -1], refs[-1]
    width = parts[0].shape[1]

    def wide(side, low, high):
        chunks, found, at = parts[sum(counts[:side]) : sum(counts[: side + 1])], [], 0
        for chunk in chunks:
            for row in range(0, chunk.shape[0], width):
                if low <= at + row < high:
                    found.append(chunk[row : row + width, :])
            at += chunk.shape[0]
        return jnp.concatenate(found, axis=1)

    for low in range(0, factors.shape[0], block):
        both = jnp.concatenate([wide(side, low, low + block) for side in range(len(counts))], axis=0)
        grown = jnp.dot(both, factors[low : low + block, :], preferred_element_type=jnp.float32)
        if low == 0:
            sums[...] = grown
        else:
            sums[...] += grown
    owned = sums.shape[1] // shards
    for hop in range(shards):
        at = pl.multiple_of(lax.rem(place[0] + hop, shards) * owned, owned)
        if joined:
            outs[hop][...] = sums[:, pl.ds(at, owned)].astype(outs[hop].dtype)
        else:
            outs[hop][...] = sums[:width, pl.ds(at, owned)].astype(outs[hop].dtype)
            outs[shards + hop][...] = sums[width:, pl.ds(at, owned)].astype(outs[shards + hop].dtype)


def gradients_of(place, factors, sides, shards, kinds, joined, block=1024):
    count, orbitals = factors.shape
    width, owned = sides[0][0].shape[1], orbitals // shards
    flat = [chunk for side in sides for chunk in side]
    rows = width * len(sides)
    if joined:
        outs = [jax.ShapeDtypeStruct((rows, owned), kind) for kind in kinds]
    else:
        outs = [jax.ShapeDtypeStruct((width, owned), kind) for kind in kinds]
    return pl.pallas_call(
        functools.partial(gradient_body, shards, [len(side) for side in sides], min(block, count), joined),
        in_specs=[pl.BlockSpec(memory_space=pltpu.SMEM)] + [pl.BlockSpec(memory_space=pltpu.VMEM)] * (1 + len(flat)),
        out_specs=[pl.BlockSpec(memory_space=pltpu.VMEM)] * len(outs),
        scratch_shapes=[pltpu.VMEM((rows, orbitals), jnp.float32)],
        out_shape=outs,
        compiler_params=SMALL,
        cost_estimate=pl.CostEstimate(flops=2 * count * orbitals * rows, transcendentals=0, bytes_accessed=2 * count * orbitals),
    )(place, factors, *flat)


def sum_body(low, refs_in, *refs):
    total = refs[0][...].astype(jnp.float32)
    for part in refs[1:refs_in]:
        total = total + part[...].astype(jnp.float32)
    if len(refs) == refs_in + 1:
        refs[-1][...] = total.astype(refs[-1].dtype)
    else:
        refs[-2][...] = total[:low]
        refs[-1][...] = total[low:].astype(jnp.bfloat16)


def sums_of(parts, split=False):
    rows, columns = parts[0].shape
    if split:
        outs = [jax.ShapeDtypeStruct((rows // 2, columns), kind) for kind in (jnp.float32, jnp.bfloat16)]
    else:
        outs = [jax.ShapeDtypeStruct((rows, columns), jnp.bfloat16)]
    return pl.pallas_call(functools.partial(sum_body, rows // 2, len(parts)), out_shape=outs, compiler_params=SMALL)(*parts)


def total_body(counts, *refs):
    out, at = refs[-1], 0
    for walker, count in enumerate(counts):
        total = refs[at][...].astype(jnp.float32)
        for part in refs[at + 1 : at + count]:
            total = total + part[...].astype(jnp.float32)
        out[walker] = -total.T
        at += count


def totals_of(pieces):
    width, owned = pieces[0][0].shape
    return pl.pallas_call(
        functools.partial(total_body, [len(walker) for walker in pieces]),
        out_shape=jax.ShapeDtypeStruct((len(pieces), owned, width), jnp.float32),
        compiler_params=SMALL,
    )(*[piece for walker in pieces for piece in walker])


def after(value, earlier):
    return lax.optimization_barrier((value, earlier))[0]


def paired(shape, chol_half, theta):
    shards = shape["vec"]
    vectors, width, orbitals = chol_half.shape
    walkers = theta.shape[0]
    factors = pltpu.with_memory_space_constraint(chol_half.reshape(vectors * width, orbitals), pltpu.VMEM)
    place = lax.axis_index("vec").reshape(1)

    def flat(grp, vec, occ, wlk):
        return ((grp * shape["vec"] + vec) * shape["occ"] + occ) * shape["wlk"] + wlk

    def moved(value, hop, across=False):
        pairs = [
            (flat(grp, vec, occ, wlk), flat(grp, (vec + hop) % shards, 1 - occ if across else occ, wlk))
            for grp in range(shape["grp"])
            for vec in range(shards)
            for occ in range(shape["occ"])
            for wlk in range(shape["wlk"])
        ]
        return lax.ppermute(value, AXES, pairs)

    last = walkers - 1
    blocks, sides = [], []

    def amplitudes(walker, cuts, ready):
        kept, received = [], []
        for low, high in zip(cuts[:-1], cuts[1:]):
            own, far = amplitudes_of(after(place, ready), factors, blocks[walker], low * width, (high - low) * width, width)
            kept.append(own)
            received.append(moved(far, 0, True))
            ready = far
        sides.append([kept, received])
        return ready

    for walker in range(walkers):
        mine = theta[walker]
        if walker == 0:
            near = [mine] + [moved(mine, hop) for hop in range(1, shards)]
            factors, near[1] = lax.optimization_barrier((factors, near[1]))
            blocks.append(near + [moved(block, 0, True) for block in near])
        else:
            both = jnp.concatenate([mine, moved(mine, 0, True)], axis=1)
            blocks.append([both] + [moved(both, hop) for hop in range(1, shards)])

    ready = place
    for walker in range(walkers):
        ready = amplitudes(walker, (0, vectors // 4, vectors) if walker == 0 else (0, vectors // 2, vectors), ready)

    pieces, ready = [], place
    for walker in range(walkers):
        kinds = [jnp.float32] + [jnp.bfloat16] * (shards - 1)
        if walker < last:
            got = gradients_of(after(place, ready), factors, sides[walker], shards, kinds, True)
            arrived = [got[0]] + [moved(got[hop], hop) for hop in range(1, shards)]
            own, far = sums_of(arrived, split=True)
            pieces.append([own, moved(far, 0, True)])
            ready = far
        else:
            got = gradients_of(after(place, ready), factors, sides[walker], shards, kinds + [jnp.bfloat16] * shards, False)
            crossed = [moved(got[shards + hop], 0, True) for hop in reversed(range(shards))][::-1]
            sent = [moved(sums_of([got[hop], crossed[hop]])[0], hop) for hop in reversed(range(1, shards))]
            pieces.append([got[0], crossed[0]] + sent)
    return totals_of(pieces)


def solution(mesh):
    placed = (P(("grp", "vec"), "occ", None), P(("grp", "wlk"), "vec", "occ"))
    on_device = functools.partial(paired, dict(mesh.shape)) if mesh.shape["occ"] == 2 else general
    return jax.shard_map(
        on_device,
        mesh=mesh,
        in_specs=placed,
        out_specs=P(("grp", "wlk"), "vec", "occ"),
        check_vma=False,
    )
```

```python
import functools

import jax
import jax.numpy as jnp
from jax import lax
from jax.experimental import pallas as pl
from jax.experimental.pallas import tpu as pltpu
from jax.sharding import PartitionSpec as P


AXES = ("grp", "vec", "occ", "wlk")
HALVES = 2
LOADS = 4
SMALL = pltpu.CompilerParams(vmem_limit_bytes=24 * 2**20)


def general(chol_half, theta):
    widened = lax.all_gather(theta, "occ", axis=2, tiled=True)
    amplitude_sums = jnp.einsum(
        "gip,wpj->wgij",
        chol_half,
        lax.all_gather(widened, "vec", axis=1, tiled=True),
        preferred_element_type=jnp.float32,
    )
    amplitudes = amplitude_sums.astype(jnp.bfloat16)
    swapped = lax.all_to_all(amplitudes, "occ", split_axis=3, concat_axis=2, tiled=True)
    summed_rows = lax.psum_scatter(
        jnp.einsum("gap,wgba->pwb", chol_half, swapped, preferred_element_type=jnp.float32),
        "vec",
        scatter_dimension=0,
        tiled=True,
    )
    owned = lax.psum_scatter(summed_rows, "occ", scatter_dimension=2, tiled=True)
    return -jnp.transpose(owned, (1, 0, 2))


VMEM = pl.BlockSpec(memory_space=pltpu.VMEM)
SMEM = pl.BlockSpec(memory_space=pltpu.SMEM)


def peer(position, hop, shards, back=False):
    if shards & (shards - 1) == 0:
        return position ^ hop
    return (position + (shards - hop if back else hop)) % shards


def load_body(first, source, out, arrived):
    copy = pltpu.make_async_copy(source.at[pl.ds(first, out.shape[0])], out, arrived)
    copy.start()
    copy.wait()


def loaded(factors, first, count):
    return pl.pallas_call(
        functools.partial(load_body, first),
        in_specs=[pl.BlockSpec(memory_space=pl.ANY)],
        out_specs=VMEM,
        out_shape=pltpu.VMEM((count, factors.shape[1]), factors.dtype),
        scratch_shapes=[pltpu.SemaphoreType.DMA],
        compiler_params=SMALL,
    )(factors)


def amplitude_body(shards, loads, half, place, *refs):
    factors, pieces, own, far, rows = refs[:loads], refs[loads:-3], refs[-3], refs[-2], refs[-1]
    owned, width = pieces[0].shape[0], own.shape[1]
    for step in range(shards):
        at = pl.multiple_of(place[step] * owned, owned)
        if len(pieces) == shards:
            rows[pl.ds(at, owned), :] = pieces[step][...]
        else:
            rows[pl.ds(at, owned), :width] = pieces[step][...]
            rows[pl.ds(at, owned), width:] = pieces[shards + step][...]
    part, at = width // HALVES, 0
    for chunk in factors:
        lows = range(half * part, chunk.shape[0], width)
        taken = jnp.concatenate([chunk[low : low + part, :] for low in lows], axis=0)
        sums = jnp.dot(taken, rows[...], preferred_element_type=jnp.float32).astype(jnp.bfloat16)
        own[at : at + sums.shape[0], :] = sums[:, :width]
        far[at : at + sums.shape[0], :] = sums[:, width:]
        at += sums.shape[0]


def amplitudes_of(place, factors, pieces, half, width, shards):
    orbitals = factors[0].shape[1]
    count = sum(chunk.shape[0] for chunk in factors) // HALVES
    return pl.pallas_call(
        functools.partial(amplitude_body, shards, len(factors), half),
        in_specs=[SMEM] + [VMEM] * (len(factors) + len(pieces)),
        out_specs=[VMEM] * 2,
        scratch_shapes=[pltpu.VMEM((orbitals, 2 * width), jnp.bfloat16)],
        out_shape=[jax.ShapeDtypeStruct((count, width), jnp.bfloat16)] * 2,
        compiler_params=SMALL,
        cost_estimate=pl.CostEstimate(flops=4 * count * orbitals * width, transcendentals=0, bytes_accessed=2 * count * orbitals),
    )(place, *factors, *pieces)


def gradient_body(shards, loads, groups, place, own, far, *refs):
    factors, outs, sums = refs[:loads], refs[loads:-1], refs[-1]
    width = own.shape[1]
    part, at = width // HALVES, 0
    for chunk in factors:
        vectors = range(at, at + chunk.shape[0] // width)
        wide = [jnp.concatenate([side[g * part : (g + 1) * part, :] for g in vectors], axis=1) for side in (own, far)]
        grown = jnp.dot(jnp.concatenate(wide, axis=0), chunk[...], preferred_element_type=jnp.float32)
        if at == 0:
            sums[...] = grown
        else:
            sums[...] += grown
        at += len(vectors)
    owned = sums.shape[1] // shards
    for hop in range(shards):
        low = pl.multiple_of(place[shards + hop] * owned, owned)
        if groups is None:
            outs[hop][...] = sums[:, pl.ds(low, owned)].astype(outs[hop].dtype)
            continue
        outs[hop][...] = sums[:part, pl.ds(low, owned)].astype(outs[hop].dtype)
        for group, hops in enumerate(groups):
            if hop in hops:
                to = hops.index(hop) * owned
                outs[shards + group][:, to : to + owned] = sums[part:, pl.ds(low, owned)].astype(jnp.bfloat16)


def gradients_of(place, factors, own, far, shards, groups=None):
    orbitals, width = factors[0].shape[1], own.shape[1]
    part, owned = width // HALVES, orbitals // shards
    rows = part if groups else 2 * part
    outs = [jax.ShapeDtypeStruct((rows, owned), jnp.bfloat16 if hop else jnp.float32) for hop in range(shards)]
    if groups:
        outs = [jax.ShapeDtypeStruct((part, owned), jnp.float32)] * shards
        outs += [jax.ShapeDtypeStruct((part, owned * len(hops)), jnp.bfloat16) for hops in groups]
    count = sum(chunk.shape[0] for chunk in factors)
    return pl.pallas_call(
        functools.partial(gradient_body, shards, len(factors), groups),
        in_specs=[SMEM] + [VMEM] * (2 + len(factors)),
        out_specs=[VMEM] * len(outs),
        scratch_shapes=[pltpu.VMEM((2 * part, orbitals), jnp.float32)],
        out_shape=outs,
        compiler_params=SMALL,
        cost_estimate=pl.CostEstimate(flops=4 * count * orbitals * part, transcendentals=0, bytes_accessed=2 * count * orbitals),
    )(place, own, far, *factors)


def split_body(*refs):
    total = refs[0][...].astype(jnp.float32)
    for part in refs[1:-2]:
        total = total + part[...].astype(jnp.float32)
    half = total.shape[0] // 2
    refs[-2][...] = total[:half]
    refs[-1][...] = total[half:].astype(jnp.bfloat16)


def split_sum(parts):
    rows, columns = parts[0].shape
    outs = [jax.ShapeDtypeStruct((rows // 2, columns), kind) for kind in (jnp.float32, jnp.bfloat16)]
    return pl.pallas_call(split_body, out_shape=outs, compiler_params=SMALL)(*parts)


def join_body(came, *refs):
    count = len(refs) // 2
    for at in range(count):
        own, out = refs[at], refs[count + at]
        columns = own.shape[1]
        out[...] = (own[...] + came[:, at * columns : (at + 1) * columns].astype(jnp.float32)).astype(out.dtype)


def join_sums(came, owns, kinds):
    outs = [jax.ShapeDtypeStruct(own.shape, kind) for own, kind in zip(owns, kinds)]
    return pl.pallas_call(join_body, out_shape=outs, compiler_params=SMALL)(came, *owns)


def total_body(counts, *refs):
    out, at = refs[-1], 0
    for walker, halves in enumerate(counts):
        rows = []
        for count in halves:
            total = refs[at][...].astype(jnp.float32)
            for part in refs[at + 1 : at + count]:
                total = total + part[...].astype(jnp.float32)
            rows.append(total)
            at += count
        out[walker] = -jnp.concatenate(rows, axis=0).T


def totals_of(pieces):
    part, owned = pieces[0][0][0].shape
    return pl.pallas_call(
        functools.partial(total_body, [[len(half) for half in walker] for walker in pieces]),
        out_shape=jax.ShapeDtypeStruct((len(pieces), owned, part * HALVES), jnp.float32),
        compiler_params=SMALL,
    )(*[piece for walker in pieces for half in walker for piece in half])


def paired(shape, chol_half, theta):
    return in_order(shape, chol_half, theta)


def in_order(shape, chol_half, theta):
    shards = shape["vec"]
    vectors, width, orbitals = chol_half.shape
    walkers = theta.shape[0]
    position = lax.axis_index("vec")
    place = jnp.stack([peer(position, hop, shards, True) for hop in range(shards)] + [peer(position, hop, shards) for hop in range(shards)])
    whole = chol_half.reshape(vectors * width, orbitals)
    factors = []
    for load in range(LOADS):
        factors.append(loaded(whole, load * vectors // LOADS * width, vectors // LOADS * width))

    def flat(grp, vec, occ, wlk):
        return ((grp * shape["vec"] + vec) * shape["occ"] + occ) * shape["wlk"] + wlk

    def moved(value, hop, across=False):
        pairs = [
            (flat(grp, vec, occ, wlk), flat(grp, peer(vec, hop, shards), 1 - occ if across else occ, wlk))
            for grp in range(shape["grp"])
            for vec in range(shards)
            for occ in range(shape["occ"])
            for wlk in range(shape["wlk"])
        ]
        return lax.ppermute(value, AXES, pairs)

    hops = range(1, shards)
    near = [theta[0]] + [moved(theta[0], hop) for hop in hops]
    across = moved(theta, 0, True)
    blocks = [near + [across[0]] + [moved(near[hop], 0, True) for hop in hops]]
    for walker in range(1, walkers):
        both = jnp.concatenate([theta[walker], across[walker]], axis=1)
        blocks.append([both] + [moved(both, hop) for hop in hops])

    stages = walkers * HALVES
    half = shards // 2
    groups = [list(range(half)), list(range(half, shards))]
    sides = []
    for stage in range(stages):
        own, far = amplitudes_of(place, factors, blocks[stage // HALVES], stage % HALVES, width, shards)
        sides.append([own, moved(far, 0, True)])

    pieces = [[] for _ in range(walkers)]
    for stage in range(stages):
        got = gradients_of(place, factors, *sides[stage], shards, groups if stage == stages - 1 else None)
        if stage < stages - 1:
            arrived = [got[0]] + [moved(got[hop], hop) for hop in hops]
            own, far = split_sum(arrived)
            pieces[stage // HALVES].append([own, moved(far, 0, True)])
        else:
            came = [moved(got[shards + at], 0, True) for at in range(len(groups))]
            owned = []
            for at, hops_of in enumerate(groups):
                owned += join_sums(came[at], [got[hop] for hop in hops_of], [jnp.bfloat16 if hop else jnp.float32 for hop in hops_of])
            pieces[stage // HALVES].append([owned[0]] + [moved(owned[hop], hop) for hop in hops])
    return totals_of(pieces)


def solution(mesh):
    placed = (P(("grp", "vec"), "occ", None), P(("grp", "wlk"), "vec", "occ"))
    pairs = mesh.shape["occ"] == 2
    return jax.shard_map(
        functools.partial(paired, dict(mesh.shape)) if pairs else general,
        mesh=mesh,
        in_specs=placed,
        out_specs=P(("grp", "wlk"), "vec", "occ"),
        check_vma=False,
    )
```

```python
import functools

import jax
import jax.numpy as jnp
from jax import lax
from jax.experimental import pallas as pl
from jax.experimental.pallas import tpu as pltpu
from jax.sharding import PartitionSpec as P


AXES = ("grp", "vec", "occ", "wlk")
HALVES = 2
LOADS = 4
LARGE = pltpu.CompilerParams(vmem_limit_bytes=44 * 2**20)
SMALL = pltpu.CompilerParams(vmem_limit_bytes=24 * 2**20)


def general(chol_half, theta):
    widened = lax.all_gather(theta, "occ", axis=2, tiled=True)
    amplitude_sums = jnp.einsum(
        "gip,wpj->wgij",
        chol_half,
        lax.all_gather(widened, "vec", axis=1, tiled=True),
        preferred_element_type=jnp.float32,
    )
    amplitudes = amplitude_sums.astype(jnp.bfloat16)
    swapped = lax.all_to_all(amplitudes, "occ", split_axis=3, concat_axis=2, tiled=True)
    summed_rows = lax.psum_scatter(
        jnp.einsum("gap,wgba->pwb", chol_half, swapped, preferred_element_type=jnp.float32),
        "vec",
        scatter_dimension=0,
        tiled=True,
    )
    owned = lax.psum_scatter(summed_rows, "occ", scatter_dimension=2, tiled=True)
    return -jnp.transpose(owned, (1, 0, 2))


VMEM = pl.BlockSpec(memory_space=pltpu.VMEM)
SMEM = pl.BlockSpec(memory_space=pltpu.SMEM)


def peer(position, hop, shards, back=False):
    if shards & (shards - 1) == 0:
        return position ^ hop
    moved = position + (shards - hop if back else hop)
    return moved % shards if isinstance(moved, int) else lax.rem(moved, shards)


def load_body(first, source, out, arrived):
    copy = pltpu.make_async_copy(source.at[pl.ds(first, out.shape[0])], out, arrived)
    copy.start()
    copy.wait()


def loaded(factors, first, count):
    return pl.pallas_call(
        functools.partial(load_body, first),
        in_specs=[pl.BlockSpec(memory_space=pltpu.HBM)],
        out_specs=VMEM,
        out_shape=pltpu.VMEM((count, factors.shape[1]), factors.dtype),
        scratch_shapes=[pltpu.SemaphoreType.DMA],
        compiler_params=LARGE,
    )(factors)


def amplitude_body(shards, loads, half, place, *refs):
    factors, pieces, own, far, rows = refs[:loads], refs[loads:-3], refs[-3], refs[-2], refs[-1]
    owned, width = pieces[0].shape[0], own.shape[1]
    for step in range(shards):
        at = pl.multiple_of(peer(place[0], step, shards, True) * owned, owned)
        if len(pieces) == shards:
            rows[pl.ds(at, owned), :] = pieces[step][...]
        else:
            rows[pl.ds(at, owned), :width] = pieces[step][...]
            rows[pl.ds(at, owned), width:] = pieces[shards + step][...]
    part, at = width // HALVES, 0
    for chunk in factors:
        lows = range(half * part, chunk.shape[0], width)
        taken = jnp.concatenate([chunk[low : low + part, :] for low in lows], axis=0)
        sums = jnp.dot(taken, rows[...], preferred_element_type=jnp.float32).astype(jnp.bfloat16)
        own[at : at + sums.shape[0], :] = sums[:, :width]
        far[at : at + sums.shape[0], :] = sums[:, width:]
        at += sums.shape[0]


def amplitudes_of(place, factors, pieces, half, width, shards):
    orbitals = factors[0].shape[1]
    count = sum(chunk.shape[0] for chunk in factors) // HALVES
    return pl.pallas_call(
        functools.partial(amplitude_body, shards, len(factors), half),
        in_specs=[SMEM] + [VMEM] * (len(factors) + len(pieces)),
        out_specs=[VMEM] * 2,
        scratch_shapes=[pltpu.VMEM((orbitals, 2 * width), jnp.bfloat16)],
        out_shape=[jax.ShapeDtypeStruct((count, width), jnp.bfloat16)] * 2,
        compiler_params=SMALL,
        cost_estimate=pl.CostEstimate(flops=4 * count * orbitals * width, transcendentals=0, bytes_accessed=2 * count * orbitals),
    )(place, *factors, *pieces)


def gradient_body(shards, loads, groups, place, own, far, *refs):
    factors, outs, sums = refs[:loads], refs[loads:-1], refs[-1]
    width = own.shape[1]
    part, at = width // HALVES, 0
    for chunk in factors:
        vectors = range(at, at + chunk.shape[0] // width)
        wide = [jnp.concatenate([side[g * part : (g + 1) * part, :] for g in vectors], axis=1) for side in (own, far)]
        grown = jnp.dot(jnp.concatenate(wide, axis=0), chunk[...], preferred_element_type=jnp.float32)
        if at == 0:
            sums[...] = grown
        else:
            sums[...] += grown
        at += len(vectors)
    owned = sums.shape[1] // shards
    for hop in range(shards):
        low = pl.multiple_of(peer(place[0], hop, shards) * owned, owned)
        if groups is None:
            outs[hop][...] = sums[:, pl.ds(low, owned)].astype(outs[hop].dtype)
            continue
        outs[hop][...] = sums[:part, pl.ds(low, owned)].astype(outs[hop].dtype)
        for group, hops in enumerate(groups):
            if hop in hops:
                to = hops.index(hop) * owned
                outs[shards + group][:, to : to + owned] = sums[part:, pl.ds(low, owned)].astype(jnp.bfloat16)


def gradients_of(place, factors, own, far, shards, groups=None):
    orbitals, width = factors[0].shape[1], own.shape[1]
    part, owned = width // HALVES, orbitals // shards
    rows = part if groups else 2 * part
    outs = [jax.ShapeDtypeStruct((rows, owned), jnp.bfloat16 if hop else jnp.float32) for hop in range(shards)]
    if groups:
        outs = [jax.ShapeDtypeStruct((part, owned), jnp.float32)] * shards
        outs += [jax.ShapeDtypeStruct((part, owned * len(hops)), jnp.bfloat16) for hops in groups]
    count = sum(chunk.shape[0] for chunk in factors)
    return pl.pallas_call(
        functools.partial(gradient_body, shards, len(factors), groups),
        in_specs=[SMEM] + [VMEM] * (2 + len(factors)),
        out_specs=[VMEM] * len(outs),
        scratch_shapes=[pltpu.VMEM((2 * part, orbitals), jnp.float32)],
        out_shape=outs,
        compiler_params=SMALL,
        cost_estimate=pl.CostEstimate(flops=4 * count * orbitals * part, transcendentals=0, bytes_accessed=2 * count * orbitals),
    )(place, own, far, *factors)


def split_body(*refs):
    total = refs[0][...].astype(jnp.float32)
    for part in refs[1:-2]:
        total = total + part[...].astype(jnp.float32)
    half = total.shape[0] // 2
    refs[-2][...] = total[:half]
    refs[-1][...] = total[half:].astype(jnp.bfloat16)


def split_sum(parts):
    rows, columns = parts[0].shape
    outs = [jax.ShapeDtypeStruct((rows // 2, columns), kind) for kind in (jnp.float32, jnp.bfloat16)]
    return pl.pallas_call(split_body, out_shape=outs, compiler_params=SMALL)(*parts)


def join_body(came, *refs):
    count = len(refs) // 2
    for at in range(count):
        own, out = refs[at], refs[count + at]
        columns = own.shape[1]
        out[...] = (own[...] + came[:, at * columns : (at + 1) * columns].astype(jnp.float32)).astype(out.dtype)


def join_sums(came, owns, kinds):
    outs = [jax.ShapeDtypeStruct(own.shape, kind) for own, kind in zip(owns, kinds)]
    return pl.pallas_call(join_body, out_shape=outs, compiler_params=SMALL)(came, *owns)


def total_body(counts, *refs):
    out, at = refs[-1], 0
    for walker, halves in enumerate(counts):
        rows = []
        for count in halves:
            total = refs[at][...].astype(jnp.float32)
            for part in refs[at + 1 : at + count]:
                total = total + part[...].astype(jnp.float32)
            rows.append(total)
            at += count
        out[walker] = -jnp.concatenate(rows, axis=0).T


def totals_of(pieces):
    part, owned = pieces[0][0][0].shape
    return pl.pallas_call(
        functools.partial(total_body, [[len(half) for half in walker] for walker in pieces]),
        out_shape=jax.ShapeDtypeStruct((len(pieces), owned, part * HALVES), jnp.float32),
        compiler_params=SMALL,
    )(*[piece for walker in pieces for half in walker for piece in half])


def paired(shape, chol_half, theta):
    return in_order(shape, chol_half, theta)


def in_order(shape, chol_half, theta):
    shards = shape["vec"]
    vectors, width, orbitals = chol_half.shape
    walkers = theta.shape[0]
    position = lax.axis_index("vec")
    place = position.reshape(1)
    whole = chol_half.reshape(vectors * width, orbitals)
    factors = []
    for load in range(LOADS):
        factors.append(loaded(whole, load * vectors // LOADS * width, vectors // LOADS * width))

    def flat(grp, vec, occ, wlk):
        return ((grp * shape["vec"] + vec) * shape["occ"] + occ) * shape["wlk"] + wlk

    def moved(value, hop, across=False):
        pairs = [
            (flat(grp, vec, occ, wlk), flat(grp, peer(vec, hop, shards), 1 - occ if across else occ, wlk))
            for grp in range(shape["grp"])
            for vec in range(shards)
            for occ in range(shape["occ"])
            for wlk in range(shape["wlk"])
        ]
        return lax.ppermute(value, AXES, pairs)

    hops = range(1, shards)
    near = [theta[0]] + [moved(theta[0], hop) for hop in hops]
    across = moved(theta, 0, True)
    blocks = [near + [across[0]] + [moved(near[hop], 0, True) for hop in hops]]
    for walker in range(1, walkers):
        both = jnp.concatenate([theta[walker], across[walker]], axis=1)
        blocks.append([both] + [moved(both, hop) for hop in hops])

    stages = walkers * HALVES
    half = shards // 2
    groups = [list(range(half)), list(range(half, shards))]
    sides = []
    for stage in range(stages):
        own, far = amplitudes_of(place, factors, blocks[stage // HALVES], stage % HALVES, width, shards)
        sides.append([own, moved(far, 0, True)])

    pieces = [[] for _ in range(walkers)]
    for stage in range(stages):
        got = gradients_of(place, factors, *sides[stage], shards, groups if stage == stages - 1 else None)
        if stage < stages - 1:
            arrived = [got[0]] + [moved(got[hop], hop) for hop in hops]
            own, far = split_sum(arrived)
            pieces[stage // HALVES].append([own, moved(far, 0, True)])
        else:
            came = [moved(got[shards + at], 0, True) for at in range(len(groups))]
            owned = []
            for at, hops_of in enumerate(groups):
                owned += join_sums(came[at], [got[hop] for hop in hops_of], [jnp.bfloat16 if hop else jnp.float32 for hop in hops_of])
            pieces[stage // HALVES].append([owned[0]] + [moved(owned[hop], hop) for hop in hops])
    return totals_of(pieces)


def solution(mesh):
    placed = (P(("grp", "vec"), "occ", None), P(("grp", "wlk"), "vec", "occ"))
    pairs = mesh.shape["occ"] == 2
    return jax.shard_map(
        functools.partial(paired, dict(mesh.shape)) if pairs else general,
        mesh=mesh,
        in_specs=placed,
        out_specs=P(("grp", "wlk"), "vec", "occ"),
        check_vma=False,
    )
```

```python
import functools

import jax
import jax.numpy as jnp
from jax import lax
from jax.experimental import pallas as pl
from jax.experimental.pallas import tpu as pltpu
from jax.sharding import PartitionSpec as P


AXES = ("grp", "vec", "occ", "wlk")
HALVES = 2
LOADS = 4
STREAMS = 4
LARGE = pltpu.CompilerParams(vmem_limit_bytes=44 * 2**20)
SMALL = pltpu.CompilerParams(vmem_limit_bytes=24 * 2**20)


def general(chol_half, theta):
    widened = lax.all_gather(theta, "occ", axis=2, tiled=True)
    amplitude_sums = jnp.einsum(
        "gip,wpj->wgij",
        chol_half,
        lax.all_gather(widened, "vec", axis=1, tiled=True),
        preferred_element_type=jnp.float32,
    )
    amplitudes = amplitude_sums.astype(jnp.bfloat16)
    swapped = lax.all_to_all(amplitudes, "occ", split_axis=3, concat_axis=2, tiled=True)
    summed_rows = lax.psum_scatter(
        jnp.einsum("gap,wgba->pwb", chol_half, swapped, preferred_element_type=jnp.float32),
        "vec",
        scatter_dimension=0,
        tiled=True,
    )
    owned = lax.psum_scatter(summed_rows, "occ", scatter_dimension=2, tiled=True)
    return -jnp.transpose(owned, (1, 0, 2))


VMEM = pl.BlockSpec(memory_space=pltpu.VMEM)
SMEM = pl.BlockSpec(memory_space=pltpu.SMEM)


def peer(position, hop, shards, back=False):
    if shards & (shards - 1) == 0:
        return position ^ hop
    moved = position + (shards - hop if back else hop)
    return moved % shards if isinstance(moved, int) else lax.rem(moved, shards)


def load_body(first, place, source, out, arrived):
    del place
    rows = out.shape[0] // STREAMS
    copies = [pltpu.make_async_copy(source.at[pl.ds(first + at * rows, rows)], out.at[pl.ds(at * rows, rows)], arrived.at[at]) for at in range(STREAMS)]
    for copy in copies:
        copy.start()
    for copy in copies:
        copy.wait()


def loaded(place, factors, first, count):
    return pl.pallas_call(
        functools.partial(load_body, first),
        in_specs=[SMEM, pl.BlockSpec(memory_space=pltpu.HBM)],
        out_specs=VMEM,
        out_shape=pltpu.VMEM((count, factors.shape[1]), factors.dtype),
        scratch_shapes=[pltpu.SemaphoreType.DMA((STREAMS,))],
        compiler_params=LARGE,
    )(place, factors)


def amplitude_body(shards, loads, half, place, *refs):
    factors, pieces, own, far, rows = refs[:loads], refs[loads:-3], refs[-3], refs[-2], refs[-1]
    owned, width = pieces[0].shape[0], own.shape[1]
    for step in range(shards):
        at = pl.multiple_of(peer(place[0], step, shards, True) * owned, owned)
        if len(pieces) == shards:
            rows[pl.ds(at, owned), :] = pieces[step][...]
        else:
            rows[pl.ds(at, owned), :width] = pieces[step][...]
            rows[pl.ds(at, owned), width:] = pieces[shards + step][...]
    part, at = width // HALVES, 0
    for chunk in factors:
        lows = range(half * part, chunk.shape[0], width)
        taken = jnp.concatenate([chunk[low : low + part, :] for low in lows], axis=0)
        sums = jnp.dot(taken, rows[...], preferred_element_type=jnp.float32).astype(jnp.bfloat16)
        own[at : at + sums.shape[0], :] = sums[:, :width]
        far[at : at + sums.shape[0], :] = sums[:, width:]
        at += sums.shape[0]


def amplitudes_of(place, factors, pieces, half, width, shards):
    orbitals = factors[0].shape[1]
    count = sum(chunk.shape[0] for chunk in factors) // HALVES
    return pl.pallas_call(
        functools.partial(amplitude_body, shards, len(factors), half),
        in_specs=[SMEM] + [VMEM] * (len(factors) + len(pieces)),
        out_specs=[VMEM] * 2,
        scratch_shapes=[pltpu.VMEM((orbitals, 2 * width), jnp.bfloat16)],
        out_shape=[jax.ShapeDtypeStruct((count, width), jnp.bfloat16)] * 2,
        compiler_params=SMALL,
        cost_estimate=pl.CostEstimate(flops=4 * count * orbitals * width, transcendentals=0, bytes_accessed=2 * count * orbitals),
    )(place, *factors, *pieces)


def gradient_body(shards, counts, carried, groups, place, *refs):
    owns, fars, factors = refs[: counts[0]], refs[counts[0] : 2 * counts[0]], refs[2 * counts[0] : 2 * counts[0] + counts[1]]
    outs, sums = refs[2 * counts[0] + counts[1] + carried : -1], refs[-1]
    width = owns[0].shape[1]
    part = width // HALVES
    slots = [(at, g) for at, own in enumerate(owns) for g in range(own.shape[0] // part)]
    seen = 0
    for chunk in factors:
        vectors = slots[seen : seen + chunk.shape[0] // width]
        wide = [jnp.concatenate([side[at][g * part : (g + 1) * part, :] for at, g in vectors], axis=1) for side in (owns, fars)]
        grown = jnp.dot(jnp.concatenate(wide, axis=0), chunk[...], preferred_element_type=jnp.float32)
        if seen == 0 and carried:
            sums[...] = refs[2 * counts[0] + counts[1]][...] + grown
        elif seen == 0:
            sums[...] = grown
        else:
            sums[...] += grown
        seen += len(vectors)
    if len(outs) == 1:
        outs[0][...] = sums[...]
        return
    owned = sums.shape[1] // shards
    for hop in range(shards):
        low = pl.multiple_of(peer(place[0], hop, shards) * owned, owned)
        if groups is None:
            outs[hop][...] = sums[:, pl.ds(low, owned)].astype(outs[hop].dtype)
            continue
        outs[hop][...] = sums[:part, pl.ds(low, owned)].astype(outs[hop].dtype)
        for group, hops in enumerate(groups):
            if hop in hops:
                to = hops.index(hop) * owned
                outs[shards + group][:, to : to + owned] = sums[part:, pl.ds(low, owned)].astype(jnp.bfloat16)


def gradients_of(place, factors, owns, fars, shards, groups=None, carried=None, more=False):
    orbitals, width = factors[0].shape[1], owns[0].shape[1]
    part, owned = width // HALVES, orbitals // shards
    outs = [jax.ShapeDtypeStruct((2 * part, owned), jnp.bfloat16 if hop else jnp.float32) for hop in range(shards)]
    if more:
        outs = [jax.ShapeDtypeStruct((2 * part, orbitals), jnp.float32)]
    elif groups:
        outs = [jax.ShapeDtypeStruct((part, owned), jnp.float32)] * shards
        outs += [jax.ShapeDtypeStruct((part, owned * len(hops)), jnp.bfloat16) for hops in groups]
    count = sum(chunk.shape[0] for chunk in factors)
    values = [place, *owns, *fars, *factors] + ([] if carried is None else [carried])
    return pl.pallas_call(
        functools.partial(gradient_body, shards, (len(owns), len(factors)), 0 if carried is None else 1, groups),
        in_specs=[SMEM] + [VMEM] * (len(values) - 1),
        out_specs=[VMEM] * len(outs),
        scratch_shapes=[pltpu.VMEM((2 * part, orbitals), jnp.float32)],
        out_shape=outs,
        compiler_params=SMALL,
        cost_estimate=pl.CostEstimate(flops=4 * count * orbitals * part, transcendentals=0, bytes_accessed=2 * count * orbitals),
    )(*values)


def split_body(each, *refs):
    inputs, outs = refs[: -(len(refs) // (each + 1)) - 1], refs[-(len(refs) // (each + 1)) - 1 :]
    for stage, own in enumerate(outs[:-1]):
        parts = inputs[stage * each : (stage + 1) * each]
        total = parts[0][...].astype(jnp.float32)
        for part in parts[1:]:
            total = total + part[...].astype(jnp.float32)
        half = own.shape[0]
        own[...] = total[:half]
        outs[-1][stage * half : (stage + 1) * half, :] = total[half:].astype(jnp.bfloat16)


def split_sums(stages):
    rows, columns = stages[0][0].shape
    outs = [jax.ShapeDtypeStruct((rows // 2, columns), jnp.float32)] * len(stages)
    outs += [jax.ShapeDtypeStruct((len(stages) * (rows // 2), columns), jnp.bfloat16)]
    flat = [part for stage in stages for part in stage]
    return pl.pallas_call(functools.partial(split_body, len(stages[0])), out_shape=outs, compiler_params=SMALL)(*flat)


def join_body(came, *refs):
    count = len(refs) // 2
    for at in range(count):
        own, out = refs[at], refs[count + at]
        columns = own.shape[1]
        out[...] = (own[...] + came[:, at * columns : (at + 1) * columns].astype(jnp.float32)).astype(out.dtype)


def join_sums(came, owns, kinds):
    outs = [jax.ShapeDtypeStruct(own.shape, kind) for own, kind in zip(owns, kinds)]
    return pl.pallas_call(join_body, out_shape=outs, compiler_params=SMALL)(came, *owns)


def total_body(plan, *refs):
    out = refs[-1]
    for walker, halves in enumerate(plan):
        rows = []
        for parts in halves:
            total = None
            for at, low, high in parts:
                value = refs[at][low:high, :].astype(jnp.float32)
                total = value if total is None else total + value
            rows.append(total)
        out[walker] = -jnp.concatenate(rows, axis=0).T


def totals_of(values, plan):
    part, owned = values[0].shape
    return pl.pallas_call(
        functools.partial(total_body, plan),
        out_shape=jax.ShapeDtypeStruct((len(plan), owned, part * HALVES), jnp.float32),
        compiler_params=SMALL,
    )(*values)


def parts_of(stage, stages):
    if stage == 0:
        return [[0], list(range(1, LOADS))]
    if stage == stages - 1:
        return [list(range(LOADS - 1)), [LOADS - 1]]
    return [list(range(LOADS))]


def paired(shape, chol_half, theta):
    return in_order(shape, chol_half, theta)


def in_order(shape, chol_half, theta):
    shards = shape["vec"]
    vectors, width, orbitals = chol_half.shape
    walkers = theta.shape[0]
    position = lax.axis_index("vec")
    place = position.reshape(1)
    whole = chol_half.reshape(vectors * width, orbitals)
    rows = vectors // LOADS * width
    factors = []
    for load in range(LOADS):
        factors.append(loaded(place, whole, load * rows, rows))

    def flat(grp, vec, occ, wlk):
        return ((grp * shape["vec"] + vec) * shape["occ"] + occ) * shape["wlk"] + wlk

    def moved(value, hop, across=False):
        pairs = [
            (flat(grp, vec, occ, wlk), flat(grp, peer(vec, hop, shards), 1 - occ if across else occ, wlk))
            for grp in range(shape["grp"])
            for vec in range(shards)
            for occ in range(shape["occ"])
            for wlk in range(shape["wlk"])
        ]
        return lax.ppermute(value, AXES, pairs)

    hops = range(1, shards)
    near = [theta[0]] + [moved(theta[0], hop) for hop in hops]
    across = moved(theta, 0, True)
    blocks = [near + [across[0]] + [moved(near[hop], 0, True) for hop in hops]]
    for walker in range(1, walkers):
        both = jnp.concatenate([theta[walker], across[walker]], axis=1)
        blocks.append([both] + [moved(both, hop) for hop in hops])

    stages = walkers * HALVES
    half = shards // 2
    groups = [list(range(half)), list(range(half, shards))]
    sides = []
    for stage in range(stages):
        owns, fars = [], []
        for loads in parts_of(stage, stages):
            own, far = amplitudes_of(place, [factors[load] for load in loads], blocks[stage // HALVES], stage % HALVES, width, shards)
            owns.append(own)
            fars.append(moved(far, 0, True))
        sides.append((owns, fars))

    arrived = []
    for stage in range(stages - 1):
        got = gradients_of(place, factors, *sides[stage], shards)
        arrived.append([got[0]] + [moved(got[hop], hop) for hop in hops])

    owns, fars = sides[-1]
    first, then = parts_of(stages - 1, stages)
    (carried,) = gradients_of(place, [factors[load] for load in first], owns[:1], fars[:1], shards, more=True)
    got = gradients_of(place, [factors[load] for load in then], owns[1:], fars[1:], shards, groups, carried)
    came = [moved(got[shards + at], 0, True) for at in range(len(groups))]
    *kept, crossing = split_sums(arrived)
    crossed = moved(crossing, 0, True)
    owned = []
    for at, hops_of in enumerate(groups):
        owned += join_sums(came[at], [got[hop] for hop in hops_of], [jnp.bfloat16 if hop else jnp.float32 for hop in hops_of])
    ends = [owned[0]] + [moved(owned[hop], hop) for hop in hops]

    part = width // HALVES
    values = [*kept, crossed, *ends]
    plan = [[(stage, 0, part), (stages - 1, stage * part, (stage + 1) * part)] for stage in range(stages - 1)]
    plan.append([(stages + at, 0, part) for at in range(len(ends))])
    return totals_of(values, [plan[walker * HALVES : (walker + 1) * HALVES] for walker in range(walkers)])


def solution(mesh):
    placed = (P(("grp", "vec"), "occ", None), P(("grp", "wlk"), "vec", "occ"))
    pairs = mesh.shape["occ"] == 2
    return jax.shard_map(
        functools.partial(paired, dict(mesh.shape)) if pairs else general,
        mesh=mesh,
        in_specs=placed,
        out_specs=P(("grp", "wlk"), "vec", "occ"),
        check_vma=False,
    )
```

```python
import functools

import jax
import jax.numpy as jnp
from jax import lax
from jax.experimental import pallas as pl
from jax.experimental.pallas import tpu as pltpu
from jax.sharding import PartitionSpec as P


AXES = ("grp", "vec", "occ", "wlk")
HALVES = 2
STREAMS = 4
BLOCK = 8
LARGE = pltpu.CompilerParams(vmem_limit_bytes=44 * 2**20)
SMALL = pltpu.CompilerParams(vmem_limit_bytes=24 * 2**20)


def general(chol_half, theta):
    widened = lax.all_gather(theta, "occ", axis=2, tiled=True)
    amplitude_sums = jnp.einsum(
        "gip,wpj->wgij",
        chol_half,
        lax.all_gather(widened, "vec", axis=1, tiled=True),
        preferred_element_type=jnp.float32,
    )
    amplitudes = amplitude_sums.astype(jnp.bfloat16)
    swapped = lax.all_to_all(amplitudes, "occ", split_axis=3, concat_axis=2, tiled=True)
    summed_rows = lax.psum_scatter(
        jnp.einsum("gap,wgba->pwb", chol_half, swapped, preferred_element_type=jnp.float32),
        "vec",
        scatter_dimension=0,
        tiled=True,
    )
    owned = lax.psum_scatter(summed_rows, "occ", scatter_dimension=2, tiled=True)
    return -jnp.transpose(owned, (1, 0, 2))


VMEM = pl.BlockSpec(memory_space=pltpu.VMEM)
SMEM = pl.BlockSpec(memory_space=pltpu.SMEM)


def peer(position, hop, shards, back=False):
    if shards & (shards - 1) == 0:
        return position ^ hop
    moved = position + (shards - hop if back else hop)
    return moved % shards if isinstance(moved, int) else lax.rem(moved, shards)


def hops_of(shards):
    return sorted(range(1, shards), key=lambda hop: (hop != shards // 2, -hop))


def groups_of(shards):
    hops = hops_of(shards) + [0]
    return [hops[: shards // 2], hops[shards // 2 :]]


def load_body(first, place, source, out, arrived):
    del place
    rows = out.shape[0] // STREAMS
    copies = [pltpu.make_async_copy(source.at[pl.ds(first + at * rows, rows)], out.at[pl.ds(at * rows, rows)], arrived.at[at]) for at in range(STREAMS)]
    for copy in copies:
        copy.start()
    for copy in copies:
        copy.wait()


def loaded(place, factors, first, count):
    return pl.pallas_call(
        functools.partial(load_body, first),
        in_specs=[SMEM, pl.BlockSpec(memory_space=pltpu.HBM)],
        out_specs=VMEM,
        out_shape=pltpu.VMEM((count, factors.shape[1]), factors.dtype),
        scratch_shapes=[pltpu.SemaphoreType.DMA((STREAMS,))],
        compiler_params=LARGE,
    )(place, factors)


def amplitude_body(shards, low, high, half, place, factors, *refs):
    pieces, own, far, rows = refs[:-3], refs[-3], refs[-2], refs[-1]
    owned, width = pieces[0].shape[0], own.shape[1]
    for step in range(shards):
        at = pl.multiple_of(peer(place[0], step, shards, True) * owned, owned)
        if len(pieces) == shards:
            rows[pl.ds(at, owned), :] = pieces[step][...]
        else:
            rows[pl.ds(at, owned), :width] = pieces[step][...]
            rows[pl.ds(at, owned), width:] = pieces[shards + step][...]
    part = width // HALVES
    for first in range(low, high, BLOCK):
        vectors = range(first, min(first + BLOCK, high))
        taken = jnp.concatenate([factors[g * width + half * part : g * width + (half + 1) * part, :] for g in vectors], axis=0)
        sums = jnp.dot(taken, rows[...], preferred_element_type=jnp.float32).astype(jnp.bfloat16)
        at = (first - low) * part
        own[at : at + sums.shape[0], :] = sums[:, :width]
        far[at : at + sums.shape[0], :] = sums[:, width:]


def amplitudes_of(place, factors, pieces, vectors, half, width, shards):
    orbitals = factors.shape[1]
    count = (vectors[1] - vectors[0]) * width // HALVES
    return pl.pallas_call(
        functools.partial(amplitude_body, shards, *vectors, half),
        in_specs=[SMEM] + [VMEM] * (1 + len(pieces)),
        out_specs=[VMEM] * 2,
        scratch_shapes=[pltpu.VMEM((orbitals, 2 * width), jnp.bfloat16)],
        out_shape=[jax.ShapeDtypeStruct((count, width), jnp.bfloat16)] * 2,
        compiler_params=SMALL,
        cost_estimate=pl.CostEstimate(flops=4 * count * orbitals * width, transcendentals=0, bytes_accessed=2 * count * orbitals),
    )(place, factors, *pieces)


def gradient_body(shards, parts, first, carried, groups, place, *refs):
    owns, fars, factors = refs[:parts], refs[parts : 2 * parts], refs[2 * parts]
    outs, sums = refs[2 * parts + 1 + carried : -1], refs[-1]
    width = owns[0].shape[1]
    part = width // HALVES
    slots = [(at, g) for at, own in enumerate(owns) for g in range(own.shape[0] // part)]
    for seen in range(0, len(slots), BLOCK):
        vectors = slots[seen : seen + BLOCK]
        wide = [jnp.concatenate([side[at][g * part : (g + 1) * part, :] for at, g in vectors], axis=1) for side in (owns, fars)]
        low = (first + seen) * width
        grown = jnp.dot(jnp.concatenate(wide, axis=0), factors[low : low + len(vectors) * width, :], preferred_element_type=jnp.float32)
        if seen == 0 and carried:
            sums[...] = refs[2 * parts + 1][...] + grown
        elif seen == 0:
            sums[...] = grown
        else:
            sums[...] += grown
    if len(outs) == 1:
        outs[0][...] = sums[...]
        return
    owned = sums.shape[1] // shards
    for hop in range(shards):
        low = pl.multiple_of(peer(place[0], hop, shards) * owned, owned)
        if groups is None:
            outs[hop][...] = sums[:, pl.ds(low, owned)].astype(outs[hop].dtype)
            continue
        outs[hop][...] = sums[:part, pl.ds(low, owned)].astype(outs[hop].dtype)
        for group, hops in enumerate(groups):
            if hop in hops:
                to = hops.index(hop) * owned
                outs[shards + group][:, to : to + owned] = sums[part:, pl.ds(low, owned)].astype(jnp.bfloat16)


def gradients_of(place, factors, owns, fars, shards, first=0, groups=None, carried=None, more=False):
    orbitals, width = factors.shape[1], owns[0].shape[1]
    part, owned = width // HALVES, orbitals // shards
    outs = [jax.ShapeDtypeStruct((2 * part, owned), jnp.bfloat16 if hop else jnp.float32) for hop in range(shards)]
    if more:
        outs = [jax.ShapeDtypeStruct((2 * part, orbitals), jnp.float32)]
    elif groups:
        outs = [jax.ShapeDtypeStruct((part, owned), jnp.float32)] * shards
        outs += [jax.ShapeDtypeStruct((part, owned * len(hops)), jnp.bfloat16) for hops in groups]
    count = sum(own.shape[0] for own in owns) * HALVES
    values = [place, *owns, *fars, factors] + ([] if carried is None else [carried])
    return pl.pallas_call(
        functools.partial(gradient_body, shards, len(owns), first, 0 if carried is None else 1, groups),
        in_specs=[SMEM] + [VMEM] * (len(values) - 1),
        out_specs=[VMEM] * len(outs),
        scratch_shapes=[pltpu.VMEM((2 * part, orbitals), jnp.float32)],
        out_shape=outs,
        compiler_params=SMALL,
        cost_estimate=pl.CostEstimate(flops=4 * count * orbitals * part, transcendentals=0, bytes_accessed=2 * count * orbitals),
    )(*values)


def split_body(each, *refs):
    inputs, outs = refs[: -(len(refs) // (each + 1)) - 1], refs[-(len(refs) // (each + 1)) - 1 :]
    for stage, own in enumerate(outs[:-1]):
        parts = inputs[stage * each : (stage + 1) * each]
        total = parts[0][...].astype(jnp.float32)
        for part in parts[1:]:
            total = total + part[...].astype(jnp.float32)
        half = own.shape[0]
        own[...] = total[:half]
        outs[-1][stage * half : (stage + 1) * half, :] = total[half:].astype(jnp.bfloat16)


def split_sums(stages):
    rows, columns = stages[0][0].shape
    outs = [jax.ShapeDtypeStruct((rows // 2, columns), jnp.float32)] * len(stages)
    outs += [jax.ShapeDtypeStruct((len(stages) * (rows // 2), columns), jnp.bfloat16)]
    flat = [part for stage in stages for part in stage]
    return pl.pallas_call(functools.partial(split_body, len(stages[0])), out_shape=outs, compiler_params=SMALL)(*flat)


def join_body(came, *refs):
    count = len(refs) // 2
    for at in range(count):
        own, out = refs[at], refs[count + at]
        columns = own.shape[1]
        out[...] = (own[...] + came[:, at * columns : (at + 1) * columns].astype(jnp.float32)).astype(out.dtype)


def join_sums(came, owns, kinds):
    outs = [jax.ShapeDtypeStruct(own.shape, kind) for own, kind in zip(owns, kinds)]
    return pl.pallas_call(join_body, out_shape=outs, compiler_params=SMALL)(came, *owns)


def total_body(plan, *refs):
    out = refs[-1]
    for walker, halves in enumerate(plan):
        rows = []
        for parts in halves:
            total = None
            for at, low, high in parts:
                value = refs[at][low:high, :].astype(jnp.float32)
                total = value if total is None else total + value
            rows.append(total)
        out[walker] = -jnp.concatenate(rows, axis=0).T


def totals_of(values, plan):
    part, owned = values[0].shape
    return pl.pallas_call(
        functools.partial(total_body, plan),
        out_shape=jax.ShapeDtypeStruct((len(plan), owned, part * HALVES), jnp.float32),
        compiler_params=SMALL,
    )(*values)


def parts_of(stage, stages, vectors):
    if stage == 0:
        return [0, vectors // 4, vectors]
    if stage == stages - 1:
        return [0, vectors - vectors // 4, vectors]
    return [0, vectors]


def paired(shape, chol_half, theta):
    return in_order(shape, chol_half, theta)


def in_order(shape, chol_half, theta):
    shards = shape["vec"]
    vectors, width, orbitals = chol_half.shape
    walkers = theta.shape[0]
    position = lax.axis_index("vec")
    place = position.reshape(1)
    whole = chol_half.reshape(vectors * width, orbitals)
    factors = loaded(place, whole, 0, vectors * width)

    def flat(grp, vec, occ, wlk):
        return ((grp * shape["vec"] + vec) * shape["occ"] + occ) * shape["wlk"] + wlk

    def moved(value, hop, across=False):
        pairs = [
            (flat(grp, vec, occ, wlk), flat(grp, peer(vec, hop, shards), 1 - occ if across else occ, wlk))
            for grp in range(shape["grp"])
            for vec in range(shards)
            for occ in range(shape["occ"])
            for wlk in range(shape["wlk"])
        ]
        return lax.ppermute(value, AXES, pairs)

    hops = range(1, shards)
    near = [theta[0]] + [moved(theta[0], hop) for hop in hops]
    across = moved(theta, 0, True)
    blocks = [near + [across[0]] + [moved(near[hop], 0, True) for hop in hops]]
    for walker in range(1, walkers):
        both = jnp.concatenate([theta[walker], across[walker]], axis=1)
        blocks.append([both] + [moved(both, hop) for hop in hops])

    stages = walkers * HALVES
    sides = []
    for stage in range(stages):
        owns, fars = [], []
        cuts = parts_of(stage, stages, vectors)
        for part in zip(cuts[:-1], cuts[1:]):
            own, far = amplitudes_of(place, factors, blocks[stage // HALVES], part, stage % HALVES, width, shards)
            owns.append(own)
            fars.append(moved(far, 0, True))
        sides.append((owns, fars))

    arrived = []
    for stage in range(stages - 1):
        got = gradients_of(place, factors, *sides[stage], shards)
        arrived.append([got[0]] + [moved(got[hop], hop) for hop in hops])
    part, values, plan = width // HALVES, [], []
    for some in (arrived[:-1], arrived[-1:]):
        *kept, crossing = split_sums(some)
        here = len(values)
        values += [*kept, moved(crossing, 0, True)]
        plan += [[(here + stage, 0, part), (here + len(kept), stage * part, (stage + 1) * part)] for stage in range(len(kept))]

    owns, fars = sides[-1]
    groups = groups_of(shards)
    (carried,) = gradients_of(place, factors, owns[:1], fars[:1], shards, more=True)
    got = gradients_of(place, factors, owns[1:], fars[1:], shards, parts_of(stages - 1, stages, vectors)[1], groups, carried)
    came = [moved(got[shards + at], 0, True) for at in range(len(groups))]
    ends = [None] * shards
    for at, group in enumerate(groups):
        joined = join_sums(came[at], [got[hop] for hop in group], [jnp.bfloat16 if hop else jnp.float32 for hop in group])
        for hop, value in zip(group, joined):
            ends[hop] = moved(value, hop) if hop else value
    plan.append([(len(values) + at, 0, part) for at in range(shards)])
    values += ends
    return totals_of(values, [plan[walker * HALVES : (walker + 1) * HALVES] for walker in range(walkers)])


def solution(mesh):
    placed = (P(("grp", "vec"), "occ", None), P(("grp", "wlk"), "vec", "occ"))
    pairs = mesh.shape["occ"] == 2
    return jax.shard_map(
        functools.partial(paired, dict(mesh.shape)) if pairs else general,
        mesh=mesh,
        in_specs=placed,
        out_specs=P(("grp", "wlk"), "vec", "occ"),
        check_vma=False,
    )
```

```python
import functools

import jax
import jax.numpy as jnp
from jax import lax
from jax.experimental import pallas as pl
from jax.experimental.pallas import tpu as pltpu
from jax.sharding import PartitionSpec as P


AXES = ("grp", "vec", "occ", "wlk")
HALVES = 2
STREAMS = 4
BLOCK = 8
LARGE = pltpu.CompilerParams(vmem_limit_bytes=44 * 2**20)
SMALL = pltpu.CompilerParams(vmem_limit_bytes=24 * 2**20)


def general(chol_half, theta):
    widened = lax.all_gather(theta, "occ", axis=2, tiled=True)
    amplitude_sums = jnp.einsum(
        "gip,wpj->wgij",
        chol_half,
        lax.all_gather(widened, "vec", axis=1, tiled=True),
        preferred_element_type=jnp.float32,
    )
    amplitudes = amplitude_sums.astype(jnp.bfloat16)
    swapped = lax.all_to_all(amplitudes, "occ", split_axis=3, concat_axis=2, tiled=True)
    summed_rows = lax.psum_scatter(
        jnp.einsum("gap,wgba->pwb", chol_half, swapped, preferred_element_type=jnp.float32),
        "vec",
        scatter_dimension=0,
        tiled=True,
    )
    owned = lax.psum_scatter(summed_rows, "occ", scatter_dimension=2, tiled=True)
    return -jnp.transpose(owned, (1, 0, 2))


VMEM = pl.BlockSpec(memory_space=pltpu.VMEM)
SMEM = pl.BlockSpec(memory_space=pltpu.SMEM)


def peer(position, hop, shards, back=False):
    if shards & (shards - 1) == 0:
        return position ^ hop
    moved = position + (shards - hop if back else hop)
    return moved % shards if isinstance(moved, int) else lax.rem(moved, shards)


def groups_of(shards):
    hops = list(range(shards - 1, -1, -1))
    return [hops[: shards // 2], hops[shards // 2 :]]


def load_body(half, place, source, out, arrived):
    del place
    vectors, part = out.shape[0] // STREAMS, out.shape[1]
    copies = []
    for at in range(STREAMS):
        some = pl.ds(at * vectors, vectors)
        copies.append(pltpu.make_async_copy(source.at[some, pl.ds(half * part, part)], out.at[some], arrived.at[at]))
    for copy in copies:
        copy.start()
    for copy in copies:
        copy.wait()


def loaded(place, factors, half):
    vectors, width, orbitals = factors.shape
    return pl.pallas_call(
        functools.partial(load_body, half),
        in_specs=[SMEM, pl.BlockSpec(memory_space=pltpu.HBM)],
        out_specs=VMEM,
        out_shape=pltpu.VMEM((vectors, width // HALVES, orbitals), factors.dtype),
        scratch_shapes=[pltpu.SemaphoreType.DMA((STREAMS,))],
        compiler_params=LARGE,
    )(place, factors)


def amplitude_body(shards, low, high, place, factors, *refs):
    pieces, own, far, rows = refs[:-3], refs[-3], refs[-2], refs[-1]
    owned, width = pieces[0].shape[0], own.shape[1]
    for step in range(shards):
        at = pl.multiple_of(peer(place[0], step, shards, True) * owned, owned)
        if len(pieces) == shards:
            rows[pl.ds(at, owned), :] = pieces[step][...]
        else:
            rows[pl.ds(at, owned), :width] = pieces[step][...]
            rows[pl.ds(at, owned), width:] = pieces[shards + step][...]
    part = factors.shape[1]
    for first in range(low, high, BLOCK):
        taken = jnp.concatenate([factors[g] for g in range(first, min(first + BLOCK, high))], axis=0)
        sums = jnp.dot(taken, rows[...], preferred_element_type=jnp.float32).astype(jnp.bfloat16)
        at = (first - low) * part
        own[at : at + sums.shape[0], :] = sums[:, :width]
        far[at : at + sums.shape[0], :] = sums[:, width:]


def amplitudes_of(place, factors, pieces, vectors, width, shards):
    orbitals = factors.shape[2]
    count = (vectors[1] - vectors[0]) * factors.shape[1]
    return pl.pallas_call(
        functools.partial(amplitude_body, shards, *vectors),
        in_specs=[SMEM] + [VMEM] * (1 + len(pieces)),
        out_specs=[VMEM] * 2,
        scratch_shapes=[pltpu.VMEM((orbitals, 2 * width), jnp.bfloat16)],
        out_shape=[jax.ShapeDtypeStruct((count, width), jnp.bfloat16)] * 2,
        compiler_params=SMALL,
        cost_estimate=pl.CostEstimate(flops=4 * count * orbitals * width, transcendentals=0, bytes_accessed=2 * count * orbitals),
    )(place, factors, *pieces)


def gradient_body(shards, parts, first, carried, groups, place, *refs):
    owns, fars, factors = refs[:parts], refs[parts : 2 * parts], refs[2 * parts : 2 * parts + HALVES]
    outs, sums = refs[2 * parts + HALVES + carried : -1], refs[-1]
    width = owns[0].shape[1]
    part = width // HALVES
    slots = [(at, g) for at, own in enumerate(owns) for g in range(own.shape[0] // part)]
    for seen in range(0, len(slots), BLOCK):
        vectors = slots[seen : seen + BLOCK]
        wide = [jnp.concatenate([side[at][g * part : (g + 1) * part, :] for at, g in vectors], axis=1) for side in (owns, fars)]
        low = first + seen
        rows = jnp.concatenate([loaded[g] for g in range(low, low + len(vectors)) for loaded in factors], axis=0)
        grown = jnp.dot(jnp.concatenate(wide, axis=0), rows, preferred_element_type=jnp.float32)
        if seen == 0 and carried:
            sums[...] = refs[2 * parts + HALVES][...] + grown
        elif seen == 0:
            sums[...] = grown
        else:
            sums[...] += grown
    if len(outs) == 1:
        outs[0][...] = sums[...]
        return
    owned = sums.shape[1] // shards
    for hop in range(shards):
        low = pl.multiple_of(peer(place[0], hop, shards) * owned, owned)
        if groups is None:
            outs[hop][...] = sums[:, pl.ds(low, owned)].astype(outs[hop].dtype)
            continue
        outs[hop][...] = sums[:part, pl.ds(low, owned)].astype(outs[hop].dtype)
        for group, hops in enumerate(groups):
            if hop in hops:
                to = hops.index(hop) * owned
                outs[shards + group][:, to : to + owned] = sums[part:, pl.ds(low, owned)].astype(jnp.bfloat16)


def gradients_of(place, factors, owns, fars, shards, first=0, groups=None, carried=None, more=False):
    orbitals, width = factors[0].shape[2], owns[0].shape[1]
    part, owned = width // HALVES, orbitals // shards
    outs = [jax.ShapeDtypeStruct((2 * part, owned), jnp.bfloat16 if hop else jnp.float32) for hop in range(shards)]
    if more:
        outs = [jax.ShapeDtypeStruct((2 * part, orbitals), jnp.float32)]
    elif groups:
        outs = [jax.ShapeDtypeStruct((part, owned), jnp.float32)] * shards
        outs += [jax.ShapeDtypeStruct((part, owned * len(hops)), jnp.bfloat16) for hops in groups]
    count = sum(own.shape[0] for own in owns) * HALVES
    values = [place, *owns, *fars, *factors] + ([] if carried is None else [carried])
    return pl.pallas_call(
        functools.partial(gradient_body, shards, len(owns), first, 0 if carried is None else 1, groups),
        in_specs=[SMEM] + [VMEM] * (len(values) - 1),
        out_specs=[VMEM] * len(outs),
        scratch_shapes=[pltpu.VMEM((2 * part, orbitals), jnp.float32)],
        out_shape=outs,
        compiler_params=SMALL,
        cost_estimate=pl.CostEstimate(flops=4 * count * orbitals * part, transcendentals=0, bytes_accessed=2 * count * orbitals),
    )(*values)


def split_body(each, *refs):
    inputs, outs = refs[: -(len(refs) // (each + 1)) - 1], refs[-(len(refs) // (each + 1)) - 1 :]
    for stage, own in enumerate(outs[:-1]):
        parts = inputs[stage * each : (stage + 1) * each]
        total = parts[0][...].astype(jnp.float32)
        for part in parts[1:]:
            total = total + part[...].astype(jnp.float32)
        half = own.shape[0]
        own[...] = total[:half]
        outs[-1][stage * half : (stage + 1) * half, :] = total[half:].astype(jnp.bfloat16)


def split_sums(stages):
    rows, columns = stages[0][0].shape
    outs = [jax.ShapeDtypeStruct((rows // 2, columns), jnp.float32)] * len(stages)
    outs += [jax.ShapeDtypeStruct((len(stages) * (rows // 2), columns), jnp.bfloat16)]
    flat = [part for stage in stages for part in stage]
    return pl.pallas_call(functools.partial(split_body, len(stages[0])), out_shape=outs, compiler_params=SMALL)(*flat)


def join_body(came, *refs):
    count = len(refs) // 2
    for at in range(count):
        own, out = refs[at], refs[count + at]
        columns = own.shape[1]
        out[...] = (own[...] + came[:, at * columns : (at + 1) * columns].astype(jnp.float32)).astype(out.dtype)


def join_sums(came, owns, kinds):
    outs = [jax.ShapeDtypeStruct(own.shape, kind) for own, kind in zip(owns, kinds)]
    return pl.pallas_call(join_body, out_shape=outs, compiler_params=SMALL)(came, *owns)


def total_body(plan, *refs):
    out = refs[-1]
    for walker, halves in enumerate(plan):
        rows = []
        for parts in halves:
            total = None
            for at, low, high in parts:
                value = refs[at][low:high, :].astype(jnp.float32)
                total = value if total is None else total + value
            rows.append(total)
        out[walker] = -jnp.concatenate(rows, axis=0).T


def totals_of(values, plan):
    part, owned = values[0].shape
    return pl.pallas_call(
        functools.partial(total_body, plan),
        out_shape=jax.ShapeDtypeStruct((len(plan), owned, part * HALVES), jnp.float32),
        compiler_params=SMALL,
    )(*values)


def parts_of(stage, stages, vectors):
    if stage == 0:
        return [0, vectors // 4, vectors]
    if stage == stages - 1:
        return [0, vectors - vectors // 4, vectors]
    return [0, vectors]


def paired(shape, chol_half, theta):
    return in_order(shape, chol_half, theta)


def in_order(shape, chol_half, theta):
    shards = shape["vec"]
    vectors, width, _ = chol_half.shape
    walkers = theta.shape[0]
    position = lax.axis_index("vec")
    place = position.reshape(1)
    factors = []
    for half in range(HALVES):
        factors.append(loaded(place, chol_half, half))

    def flat(grp, vec, occ, wlk):
        return ((grp * shape["vec"] + vec) * shape["occ"] + occ) * shape["wlk"] + wlk

    def moved(value, hop, across=False):
        pairs = [
            (flat(grp, vec, occ, wlk), flat(grp, peer(vec, hop, shards), 1 - occ if across else occ, wlk))
            for grp in range(shape["grp"])
            for vec in range(shards)
            for occ in range(shape["occ"])
            for wlk in range(shape["wlk"])
        ]
        return lax.ppermute(value, AXES, pairs)

    hops = range(1, shards)
    near = [theta[0]] + [moved(theta[0], hop) for hop in hops]
    across = moved(theta, 0, True)
    blocks = [near + [across[0]] + [moved(near[hop], 0, True) for hop in hops]]
    for walker in range(1, walkers):
        both = jnp.concatenate([theta[walker], across[walker]], axis=1)
        blocks.append([both] + [moved(both, hop) for hop in hops])

    stages = walkers * HALVES
    sides = []
    for stage in range(stages):
        owns, fars = [], []
        cuts = parts_of(stage, stages, vectors)
        for part in zip(cuts[:-1], cuts[1:]):
            own, far = amplitudes_of(place, factors[stage % HALVES], blocks[stage // HALVES], part, width, shards)
            owns.append(own)
            fars.append(moved(far, 0, True))
        sides.append((owns, fars))

    arrived = []
    for stage in range(stages - 1):
        got = gradients_of(place, factors, *sides[stage], shards)
        arrived.append([got[0]] + [moved(got[hop], hop) for hop in hops])
    part, values, plan = width // HALVES, [], []
    for some in (arrived[:-1], arrived[-1:]):
        *kept, crossing = split_sums(some)
        here = len(values)
        values += [*kept, moved(crossing, 0, True)]
        plan += [[(here + stage, 0, part), (here + len(kept), stage * part, (stage + 1) * part)] for stage in range(len(kept))]

    owns, fars = sides[-1]
    groups = groups_of(shards)
    (carried,) = gradients_of(place, factors, owns[:1], fars[:1], shards, more=True)
    got = gradients_of(place, factors, owns[1:], fars[1:], shards, parts_of(stages - 1, stages, vectors)[1], groups, carried)
    came = [moved(got[shards + at], 0, True) for at in range(len(groups))]
    ends = [None] * shards
    for at, group in enumerate(groups):
        joined = join_sums(came[at], [got[hop] for hop in group], [jnp.bfloat16 if hop else jnp.float32 for hop in group])
        for hop, value in zip(group, joined):
            ends[hop] = moved(value, hop) if hop else value
    plan.append([(len(values) + at, 0, part) for at in range(shards)])
    values += ends
    return totals_of(values, [plan[walker * HALVES : (walker + 1) * HALVES] for walker in range(walkers)])


def solution(mesh):
    placed = (P(("grp", "vec"), "occ", None), P(("grp", "wlk"), "vec", "occ"))
    pairs = mesh.shape["occ"] == 2
    return jax.shard_map(
        functools.partial(paired, dict(mesh.shape)) if pairs else general,
        mesh=mesh,
        in_specs=placed,
        out_specs=P(("grp", "wlk"), "vec", "occ"),
        check_vma=False,
    )
```

```python
import functools

import jax
import jax.numpy as jnp
from jax import lax
from jax.experimental import pallas as pl
from jax.experimental.pallas import tpu as pltpu
from jax.sharding import PartitionSpec as P


AXES = ("grp", "vec", "occ", "wlk")
HALVES = 2
STREAMS = 4
BLOCK = 8
LARGE = pltpu.CompilerParams(vmem_limit_bytes=44 * 2**20)
SMALL = pltpu.CompilerParams(vmem_limit_bytes=24 * 2**20)


def general(chol_half, theta):
    widened = lax.all_gather(theta, "occ", axis=2, tiled=True)
    amplitude_sums = jnp.einsum(
        "gip,wpj->wgij",
        chol_half,
        lax.all_gather(widened, "vec", axis=1, tiled=True),
        preferred_element_type=jnp.float32,
    )
    amplitudes = amplitude_sums.astype(jnp.bfloat16)
    swapped = lax.all_to_all(amplitudes, "occ", split_axis=3, concat_axis=2, tiled=True)
    summed_rows = lax.psum_scatter(
        jnp.einsum("gap,wgba->pwb", chol_half, swapped, preferred_element_type=jnp.float32),
        "vec",
        scatter_dimension=0,
        tiled=True,
    )
    owned = lax.psum_scatter(summed_rows, "occ", scatter_dimension=2, tiled=True)
    return -jnp.transpose(owned, (1, 0, 2))


VMEM = pl.BlockSpec(memory_space=pltpu.VMEM)
SMEM = pl.BlockSpec(memory_space=pltpu.SMEM)


def peer(position, hop, shards, back=False):
    if shards & (shards - 1) == 0:
        return position ^ hop
    moved = position + (shards - hop if back else hop)
    return moved % shards if isinstance(moved, int) else lax.rem(moved, shards)


def load_body(half, place, source, out, arrived):
    del place
    vectors, part = out.shape[0] // STREAMS, out.shape[1]
    copies = []
    for at in range(STREAMS):
        some = pl.ds(at * vectors, vectors)
        copies.append(pltpu.make_async_copy(source.at[some, pl.ds(half * part, part)], out.at[some], arrived.at[at]))
    for copy in copies:
        copy.start()
    for copy in copies:
        copy.wait()


def loaded(place, factors, half):
    vectors, width, orbitals = factors.shape
    return pl.pallas_call(
        functools.partial(load_body, half),
        in_specs=[SMEM, pl.BlockSpec(memory_space=pltpu.HBM)],
        out_specs=VMEM,
        out_shape=pltpu.VMEM((vectors, width // HALVES, orbitals), factors.dtype),
        scratch_shapes=[pltpu.SemaphoreType.DMA((STREAMS,))],
        compiler_params=LARGE,
    )(place, factors)


def amplitude_body(shards, low, high, place, factors, *refs):
    pieces, own, far, rows = refs[:-3], refs[-3], refs[-2], refs[-1]
    owned, width = pieces[0].shape[0], own.shape[1]
    for step in range(shards):
        at = pl.multiple_of(peer(place[0], step, shards, True) * owned, owned)
        if len(pieces) == shards:
            rows[pl.ds(at, owned), :] = pieces[step][...]
        else:
            rows[pl.ds(at, owned), :width] = pieces[step][...]
            rows[pl.ds(at, owned), width:] = pieces[shards + step][...]
    part = factors.shape[1]
    for first in range(low, high, BLOCK):
        taken = jnp.concatenate([factors[g] for g in range(first, min(first + BLOCK, high))], axis=0)
        sums = jnp.dot(taken, rows[...], preferred_element_type=jnp.float32).astype(jnp.bfloat16)
        at = (first - low) * part
        own[at : at + sums.shape[0], :] = sums[:, :width]
        far[at : at + sums.shape[0], :] = sums[:, width:]


def amplitudes_of(place, factors, pieces, vectors, width, shards):
    orbitals = factors.shape[2]
    count = (vectors[1] - vectors[0]) * factors.shape[1]
    return pl.pallas_call(
        functools.partial(amplitude_body, shards, *vectors),
        in_specs=[SMEM] + [VMEM] * (1 + len(pieces)),
        out_specs=[VMEM] * 2,
        scratch_shapes=[pltpu.VMEM((orbitals, 2 * width), jnp.bfloat16)],
        out_shape=[jax.ShapeDtypeStruct((count, width), jnp.bfloat16)] * 2,
        compiler_params=SMALL,
        cost_estimate=pl.CostEstimate(flops=4 * count * orbitals * width, transcendentals=0, bytes_accessed=2 * count * orbitals),
    )(place, factors, *pieces)


def gradient_body(shards, parts, first, carried, crossing, place, *refs):
    owns, fars, factors = refs[:parts], refs[parts : 2 * parts], refs[2 * parts : 2 * parts + HALVES]
    outs, sums = refs[2 * parts + HALVES + carried : -1], refs[-1]
    width = owns[0].shape[1]
    part = width // HALVES
    slots = [(at, g) for at, own in enumerate(owns) for g in range(own.shape[0] // part)]
    for seen in range(0, len(slots), BLOCK):
        vectors = slots[seen : seen + BLOCK]
        wide = [jnp.concatenate([side[at][g * part : (g + 1) * part, :] for at, g in vectors], axis=1) for side in (owns, fars)]
        low = first + seen
        rows = jnp.concatenate([loaded[g] for g in range(low, low + len(vectors)) for loaded in factors], axis=0)
        grown = jnp.dot(jnp.concatenate(wide, axis=0), rows, preferred_element_type=jnp.float32)
        if seen == 0 and carried:
            sums[...] = refs[2 * parts + HALVES][...] + grown
        elif seen == 0:
            sums[...] = grown
        else:
            sums[...] += grown
    if len(outs) == 1:
        outs[0][...] = sums[...]
        return
    owned = sums.shape[1] // shards
    for hop in range(shards):
        low = pl.multiple_of(peer(place[0], hop, shards) * owned, owned)
        if crossing:
            outs[hop][...] = sums[:part, pl.ds(low, owned)]
            outs[shards][:, hop * owned : (hop + 1) * owned] = sums[part:, pl.ds(low, owned)].astype(jnp.bfloat16)
        else:
            outs[hop][...] = sums[:, pl.ds(low, owned)].astype(outs[hop].dtype)


def gradients_of(place, factors, owns, fars, shards, first=0, crossing=False, carried=None, more=False):
    orbitals, width = factors[0].shape[2], owns[0].shape[1]
    part, owned = width // HALVES, orbitals // shards
    outs = [jax.ShapeDtypeStruct((2 * part, owned), jnp.bfloat16 if hop else jnp.float32) for hop in range(shards)]
    if more:
        outs = [jax.ShapeDtypeStruct((2 * part, orbitals), jnp.float32)]
    elif crossing:
        outs = [jax.ShapeDtypeStruct((part, owned), jnp.float32)] * shards + [jax.ShapeDtypeStruct((part, orbitals), jnp.bfloat16)]
    count = sum(own.shape[0] for own in owns) * HALVES
    values = [place, *owns, *fars, *factors] + ([] if carried is None else [carried])
    return pl.pallas_call(
        functools.partial(gradient_body, shards, len(owns), first, 0 if carried is None else 1, crossing),
        in_specs=[SMEM] + [VMEM] * (len(values) - 1),
        out_specs=[VMEM] * len(outs),
        scratch_shapes=[pltpu.VMEM((2 * part, orbitals), jnp.float32)],
        out_shape=outs,
        compiler_params=SMALL,
        cost_estimate=pl.CostEstimate(flops=4 * count * orbitals * part, transcendentals=0, bytes_accessed=2 * count * orbitals),
    )(*values)


def split_body(each, *refs):
    inputs, outs = refs[: -(len(refs) // (each + 1)) - 1], refs[-(len(refs) // (each + 1)) - 1 :]
    for stage, own in enumerate(outs[:-1]):
        parts = inputs[stage * each : (stage + 1) * each]
        total = parts[0][...].astype(jnp.float32)
        for part in parts[1:]:
            total = total + part[...].astype(jnp.float32)
        half = own.shape[0]
        own[...] = total[:half]
        outs[-1][stage * half : (stage + 1) * half, :] = total[half:].astype(jnp.bfloat16)


def split_sums(stages):
    rows, columns = stages[0][0].shape
    outs = [jax.ShapeDtypeStruct((rows // 2, columns), jnp.float32)] * len(stages)
    outs += [jax.ShapeDtypeStruct((len(stages) * (rows // 2), columns), jnp.bfloat16)]
    flat = [part for stage in stages for part in stage]
    return pl.pallas_call(functools.partial(split_body, len(stages[0])), out_shape=outs, compiler_params=SMALL)(*flat)


def join_body(came, *refs):
    count = len(refs) // 2
    for at in range(count):
        own, out = refs[at], refs[count + at]
        columns = own.shape[1]
        out[...] = (own[...] + came[:, at * columns : (at + 1) * columns].astype(jnp.float32)).astype(out.dtype)


def join_sums(came, owns, kinds):
    outs = [jax.ShapeDtypeStruct(own.shape, kind) for own, kind in zip(owns, kinds)]
    return pl.pallas_call(join_body, out_shape=outs, compiler_params=SMALL)(came, *owns)


def total_body(plan, *refs):
    out = refs[-1]
    for walker, halves in enumerate(plan):
        rows = []
        for parts in halves:
            total = None
            for at, low, high in parts:
                value = refs[at][low:high, :].astype(jnp.float32)
                total = value if total is None else total + value
            rows.append(total)
        out[walker] = -jnp.concatenate(rows, axis=0).T


def totals_of(values, plan):
    part, owned = values[0].shape
    return pl.pallas_call(
        functools.partial(total_body, plan),
        out_shape=jax.ShapeDtypeStruct((len(plan), owned, part * HALVES), jnp.float32),
        compiler_params=SMALL,
    )(*values)


def parts_of(stage, stages, vectors):
    if stage == 0:
        return [0, vectors // 4, vectors]
    if stage == stages - 1:
        return [0, vectors - vectors // 4, vectors]
    return [0, vectors]


def paired(shape, chol_half, theta):
    return in_order(shape, chol_half, theta)


def in_order(shape, chol_half, theta):
    shards = shape["vec"]
    vectors, width, _ = chol_half.shape
    walkers = theta.shape[0]
    position = lax.axis_index("vec")
    place = position.reshape(1)
    factors = []
    for half in range(HALVES):
        factors.append(loaded(place, chol_half, half))

    def flat(grp, vec, occ, wlk):
        return ((grp * shape["vec"] + vec) * shape["occ"] + occ) * shape["wlk"] + wlk

    def moved(value, hop, across=False):
        pairs = [
            (flat(grp, vec, occ, wlk), flat(grp, peer(vec, hop, shards), 1 - occ if across else occ, wlk))
            for grp in range(shape["grp"])
            for vec in range(shards)
            for occ in range(shape["occ"])
            for wlk in range(shape["wlk"])
        ]
        return lax.ppermute(value, AXES, pairs)

    hops = range(1, shards)
    near = [theta[0]] + [moved(theta[0], hop) for hop in hops]
    across = moved(theta, 0, True)
    blocks = [near + [across[0]] + [moved(near[hop], 0, True) for hop in hops]]
    for walker in range(1, walkers):
        both = jnp.concatenate([theta[walker], across[walker]], axis=1)
        blocks.append([both] + [moved(both, hop) for hop in hops])

    stages = walkers * HALVES
    sides = []
    for stage in range(stages):
        owns, fars = [], []
        cuts = parts_of(stage, stages, vectors)
        for part in zip(cuts[:-1], cuts[1:]):
            own, far = amplitudes_of(place, factors[stage % HALVES], blocks[stage // HALVES], part, width, shards)
            owns.append(own)
            fars.append(moved(far, 0, True))
        sides.append((owns, fars))

    arrived = []
    for stage in range(stages - 1):
        got = gradients_of(place, factors, *sides[stage], shards)
        arrived.append([got[0]] + [moved(got[hop], hop) for hop in hops])
    *kept, crossing = split_sums(arrived)
    part = width // HALVES
    values = [*kept, moved(crossing, 0, True)]
    plan = [[(stage, 0, part), (len(kept), stage * part, (stage + 1) * part)] for stage in range(len(kept))]

    owns, fars = sides[-1]
    (carried,) = gradients_of(place, factors, owns[:1], fars[:1], shards, more=True)
    *own, far = gradients_of(place, factors, owns[1:], fars[1:], shards, parts_of(stages - 1, stages, vectors)[1], True, carried)
    came = moved(far, 0, True)
    joined = join_sums(came, own, [jnp.bfloat16 if hop else jnp.float32 for hop in range(shards)])
    ends = [moved(value, hop) if hop else value for hop, value in enumerate(joined)]
    plan.append([(len(values) + at, 0, part) for at in range(shards)])
    values += ends
    return totals_of(values, [plan[walker * HALVES : (walker + 1) * HALVES] for walker in range(walkers)])


def solution(mesh):
    placed = (P(("grp", "vec"), "occ", None), P(("grp", "wlk"), "vec", "occ"))
    pairs = mesh.shape["occ"] == 2
    return jax.shard_map(
        functools.partial(paired, dict(mesh.shape)) if pairs else general,
        mesh=mesh,
        in_specs=placed,
        out_specs=P(("grp", "wlk"), "vec", "occ"),
        check_vma=False,
    )
```

```python
import functools

import jax
import jax.numpy as jnp
from jax import lax
from jax.experimental import pallas as pl
from jax.experimental.pallas import tpu as pltpu
from jax.sharding import PartitionSpec as P


AXES = ("grp", "vec", "occ", "wlk")
HALVES = 2
STREAMS = 4
BLOCK = 8
LARGE = pltpu.CompilerParams(vmem_limit_bytes=44 * 2**20)
SMALL = pltpu.CompilerParams(vmem_limit_bytes=24 * 2**20)


def general(chol_half, theta):
    widened = lax.all_gather(theta, "occ", axis=2, tiled=True)
    amplitude_sums = jnp.einsum(
        "gip,wpj->wgij",
        chol_half,
        lax.all_gather(widened, "vec", axis=1, tiled=True),
        preferred_element_type=jnp.float32,
    )
    amplitudes = amplitude_sums.astype(jnp.bfloat16)
    swapped = lax.all_to_all(amplitudes, "occ", split_axis=3, concat_axis=2, tiled=True)
    summed_rows = lax.psum_scatter(
        jnp.einsum("gap,wgba->pwb", chol_half, swapped, preferred_element_type=jnp.float32),
        "vec",
        scatter_dimension=0,
        tiled=True,
    )
    owned = lax.psum_scatter(summed_rows, "occ", scatter_dimension=2, tiled=True)
    return -jnp.transpose(owned, (1, 0, 2))


VMEM = pl.BlockSpec(memory_space=pltpu.VMEM)
SMEM = pl.BlockSpec(memory_space=pltpu.SMEM)


def peer(position, hop, shards, back=False):
    if shards & (shards - 1) == 0:
        return position ^ hop
    moved = position + (shards - hop if back else hop)
    return moved % shards if isinstance(moved, int) else lax.rem(moved, shards)


def groups_of(shards):
    hops = list(range(shards - 1, -1, -1))
    return [hops[:1], hops[1:]]


def load_body(half, place, source, out, arrived):
    del place
    vectors, part = out.shape[0] // STREAMS, out.shape[1]
    copies = []
    for at in range(STREAMS):
        some = pl.ds(at * vectors, vectors)
        copies.append(pltpu.make_async_copy(source.at[some, pl.ds(half * part, part)], out.at[some], arrived.at[at]))
    for copy in copies:
        copy.start()
    for copy in copies:
        copy.wait()


def loaded(place, factors, half):
    vectors, width, orbitals = factors.shape
    return pl.pallas_call(
        functools.partial(load_body, half),
        in_specs=[SMEM, pl.BlockSpec(memory_space=pltpu.HBM)],
        out_specs=VMEM,
        out_shape=pltpu.VMEM((vectors, width // HALVES, orbitals), factors.dtype),
        scratch_shapes=[pltpu.SemaphoreType.DMA((STREAMS,))],
        compiler_params=LARGE,
    )(place, factors)


def amplitude_body(shards, low, high, place, factors, *refs):
    pieces, own, far, rows = refs[:-3], refs[-3], refs[-2], refs[-1]
    owned, width = pieces[0].shape[0], own.shape[1]
    for step in range(shards):
        at = pl.multiple_of(peer(place[0], step, shards, True) * owned, owned)
        if len(pieces) == shards:
            rows[pl.ds(at, owned), :] = pieces[step][...]
        else:
            rows[pl.ds(at, owned), :width] = pieces[step][...]
            rows[pl.ds(at, owned), width:] = pieces[shards + step][...]
    part = factors.shape[1]
    for first in range(low, high, BLOCK):
        taken = jnp.concatenate([factors[g] for g in range(first, min(first + BLOCK, high))], axis=0)
        sums = jnp.dot(taken, rows[...], preferred_element_type=jnp.float32).astype(jnp.bfloat16)
        at = (first - low) * part
        own[at : at + sums.shape[0], :] = sums[:, :width]
        far[at : at + sums.shape[0], :] = sums[:, width:]


def amplitudes_of(place, factors, pieces, vectors, width, shards):
    orbitals = factors.shape[2]
    count = (vectors[1] - vectors[0]) * factors.shape[1]
    return pl.pallas_call(
        functools.partial(amplitude_body, shards, *vectors),
        in_specs=[SMEM] + [VMEM] * (1 + len(pieces)),
        out_specs=[VMEM] * 2,
        scratch_shapes=[pltpu.VMEM((orbitals, 2 * width), jnp.bfloat16)],
        out_shape=[jax.ShapeDtypeStruct((count, width), jnp.bfloat16)] * 2,
        compiler_params=SMALL,
        cost_estimate=pl.CostEstimate(flops=4 * count * orbitals * width, transcendentals=0, bytes_accessed=2 * count * orbitals),
    )(place, factors, *pieces)


def gradient_body(shards, parts, first, carried, groups, place, *refs):
    owns, fars, factors = refs[:parts], refs[parts : 2 * parts], refs[2 * parts : 2 * parts + HALVES]
    outs, sums = refs[2 * parts + HALVES + carried : -1], refs[-1]
    width = owns[0].shape[1]
    part = width // HALVES
    slots = [(at, g) for at, own in enumerate(owns) for g in range(own.shape[0] // part)]
    for seen in range(0, len(slots), BLOCK):
        vectors = slots[seen : seen + BLOCK]
        wide = [jnp.concatenate([side[at][g * part : (g + 1) * part, :] for at, g in vectors], axis=1) for side in (owns, fars)]
        low = first + seen
        rows = jnp.concatenate([loaded[g] for g in range(low, low + len(vectors)) for loaded in factors], axis=0)
        grown = jnp.dot(jnp.concatenate(wide, axis=0), rows, preferred_element_type=jnp.float32)
        if seen == 0 and carried:
            sums[...] = refs[2 * parts + HALVES][...] + grown
        elif seen == 0:
            sums[...] = grown
        else:
            sums[...] += grown
    if len(outs) == 1:
        outs[0][...] = sums[...]
        return
    owned = sums.shape[1] // shards
    for hop in range(shards):
        low = pl.multiple_of(peer(place[0], hop, shards) * owned, owned)
        if groups is None:
            outs[hop][...] = sums[:, pl.ds(low, owned)].astype(outs[hop].dtype)
            continue
        outs[hop][...] = sums[:part, pl.ds(low, owned)].astype(outs[hop].dtype)
        for group, hops in enumerate(groups):
            if hop in hops:
                to = hops.index(hop) * owned
                outs[shards + group][:, to : to + owned] = sums[part:, pl.ds(low, owned)].astype(jnp.bfloat16)


def gradients_of(place, factors, owns, fars, shards, first=0, groups=None, carried=None, more=False):
    orbitals, width = factors[0].shape[2], owns[0].shape[1]
    part, owned = width // HALVES, orbitals // shards
    outs = [jax.ShapeDtypeStruct((2 * part, owned), jnp.bfloat16 if hop else jnp.float32) for hop in range(shards)]
    if more:
        outs = [jax.ShapeDtypeStruct((2 * part, orbitals), jnp.float32)]
    elif groups:
        outs = [jax.ShapeDtypeStruct((part, owned), jnp.float32)] * shards
        outs += [jax.ShapeDtypeStruct((part, owned * len(hops)), jnp.bfloat16) for hops in groups]
    count = sum(own.shape[0] for own in owns) * HALVES
    values = [place, *owns, *fars, *factors] + ([] if carried is None else [carried])
    return pl.pallas_call(
        functools.partial(gradient_body, shards, len(owns), first, 0 if carried is None else 1, groups),
        in_specs=[SMEM] + [VMEM] * (len(values) - 1),
        out_specs=[VMEM] * len(outs),
        scratch_shapes=[pltpu.VMEM((2 * part, orbitals), jnp.float32)],
        out_shape=outs,
        compiler_params=SMALL,
        cost_estimate=pl.CostEstimate(flops=4 * count * orbitals * part, transcendentals=0, bytes_accessed=2 * count * orbitals),
    )(*values)


def split_body(each, *refs):
    inputs, outs = refs[: -(len(refs) // (each + 1)) - 1], refs[-(len(refs) // (each + 1)) - 1 :]
    for stage, own in enumerate(outs[:-1]):
        parts = inputs[stage * each : (stage + 1) * each]
        total = parts[0][...].astype(jnp.float32)
        for part in parts[1:]:
            total = total + part[...].astype(jnp.float32)
        half = own.shape[0]
        own[...] = total[:half]
        outs[-1][stage * half : (stage + 1) * half, :] = total[half:].astype(jnp.bfloat16)


def split_sums(stages):
    rows, columns = stages[0][0].shape
    outs = [jax.ShapeDtypeStruct((rows // 2, columns), jnp.float32)] * len(stages)
    outs += [jax.ShapeDtypeStruct((len(stages) * (rows // 2), columns), jnp.bfloat16)]
    flat = [part for stage in stages for part in stage]
    return pl.pallas_call(functools.partial(split_body, len(stages[0])), out_shape=outs, compiler_params=SMALL)(*flat)


def join_body(came, *refs):
    count = len(refs) // 2
    for at in range(count):
        own, out = refs[at], refs[count + at]
        columns = own.shape[1]
        out[...] = (own[...] + came[:, at * columns : (at + 1) * columns].astype(jnp.float32)).astype(out.dtype)


def join_sums(came, owns, kinds):
    outs = [jax.ShapeDtypeStruct(own.shape, kind) for own, kind in zip(owns, kinds)]
    return pl.pallas_call(join_body, out_shape=outs, compiler_params=SMALL)(came, *owns)


def total_body(plan, *refs):
    out = refs[-1]
    for walker, halves in enumerate(plan):
        rows = []
        for parts in halves:
            total = None
            for at, low, high in parts:
                value = refs[at][low:high, :].astype(jnp.float32)
                total = value if total is None else total + value
            rows.append(total)
        out[walker] = -jnp.concatenate(rows, axis=0).T


def totals_of(values, plan):
    part, owned = values[0].shape
    return pl.pallas_call(
        functools.partial(total_body, plan),
        out_shape=jax.ShapeDtypeStruct((len(plan), owned, part * HALVES), jnp.float32),
        compiler_params=SMALL,
    )(*values)


def parts_of(stage, stages, vectors):
    if stage == 0:
        return [0, vectors // 4, vectors]
    if stage == stages - 1:
        return [0, vectors - vectors // 4, vectors]
    return [0, vectors]


def paired(shape, chol_half, theta):
    return in_order(shape, chol_half, theta)


def in_order(shape, chol_half, theta):
    shards = shape["vec"]
    vectors, width, _ = chol_half.shape
    walkers = theta.shape[0]
    position = lax.axis_index("vec")
    place = position.reshape(1)
    factors = []
    for half in range(HALVES):
        factors.append(loaded(place, chol_half, half))

    def flat(grp, vec, occ, wlk):
        return ((grp * shape["vec"] + vec) * shape["occ"] + occ) * shape["wlk"] + wlk

    def moved(value, hop, across=False):
        pairs = [
            (flat(grp, vec, occ, wlk), flat(grp, peer(vec, hop, shards), 1 - occ if across else occ, wlk))
            for grp in range(shape["grp"])
            for vec in range(shards)
            for occ in range(shape["occ"])
            for wlk in range(shape["wlk"])
        ]
        return lax.ppermute(value, AXES, pairs)

    hops = range(1, shards)
    near = [theta[0]] + [moved(theta[0], hop) for hop in hops]
    across = moved(theta, 0, True)
    blocks = [near + [across[0]] + [moved(near[hop], 0, True) for hop in hops]]
    for walker in range(1, walkers):
        both = jnp.concatenate([theta[walker], across[walker]], axis=1)
        blocks.append([both] + [moved(both, hop) for hop in hops])

    stages = walkers * HALVES
    sides = []
    for stage in range(stages):
        owns, fars = [], []
        cuts = parts_of(stage, stages, vectors)
        for part in zip(cuts[:-1], cuts[1:]):
            own, far = amplitudes_of(place, factors[stage % HALVES], blocks[stage // HALVES], part, width, shards)
            owns.append(own)
            fars.append(moved(far, 0, True))
        sides.append((owns, fars))

    arrived = []
    for stage in range(stages - 1):
        got = gradients_of(place, factors, *sides[stage], shards)
        arrived.append([got[0]] + [moved(got[hop], hop) for hop in hops])
    *kept, crossing = split_sums(arrived)
    part = width // HALVES
    values = [*kept, moved(crossing, 0, True)]
    plan = [[(stage, 0, part), (len(kept), stage * part, (stage + 1) * part)] for stage in range(len(kept))]

    owns, fars = sides[-1]
    groups = groups_of(shards)
    (carried,) = gradients_of(place, factors, owns[:1], fars[:1], shards, more=True)
    got = gradients_of(place, factors, owns[1:], fars[1:], shards, parts_of(stages - 1, stages, vectors)[1], groups, carried)
    came = [moved(got[shards + at], 0, True) for at in range(len(groups))]
    ends = [None] * shards
    for at, group in enumerate(groups):
        joined = join_sums(came[at], [got[hop] for hop in group], [jnp.bfloat16 if hop else jnp.float32 for hop in group])
        for hop, value in zip(group, joined):
            ends[hop] = moved(value, hop) if hop else value
    plan.append([(len(values) + at, 0, part) for at in range(shards)])
    values += ends
    return totals_of(values, [plan[walker * HALVES : (walker + 1) * HALVES] for walker in range(walkers)])


def solution(mesh):
    placed = (P(("grp", "vec"), "occ", None), P(("grp", "wlk"), "vec", "occ"))
    pairs = mesh.shape["occ"] == 2
    return jax.shard_map(
        functools.partial(paired, dict(mesh.shape)) if pairs else general,
        mesh=mesh,
        in_specs=placed,
        out_specs=P(("grp", "wlk"), "vec", "occ"),
        check_vma=False,
    )
```

```python
import functools

import jax
import jax.numpy as jnp
from jax import lax
from jax.experimental import pallas as pl
from jax.experimental.pallas import tpu as pltpu
from jax.sharding import PartitionSpec as P


AXES = ("grp", "vec", "occ", "wlk")
HALVES = 2
STREAMS = 4
BLOCK = 8
LARGE = pltpu.CompilerParams(vmem_limit_bytes=44 * 2**20)
SMALL = pltpu.CompilerParams(vmem_limit_bytes=24 * 2**20)


def general(chol_half, theta):
    widened = lax.all_gather(theta, "occ", axis=2, tiled=True)
    amplitude_sums = jnp.einsum(
        "gip,wpj->wgij",
        chol_half,
        lax.all_gather(widened, "vec", axis=1, tiled=True),
        preferred_element_type=jnp.float32,
    )
    amplitudes = amplitude_sums.astype(jnp.bfloat16)
    swapped = lax.all_to_all(amplitudes, "occ", split_axis=3, concat_axis=2, tiled=True)
    summed_rows = lax.psum_scatter(
        jnp.einsum("gap,wgba->pwb", chol_half, swapped, preferred_element_type=jnp.float32),
        "vec",
        scatter_dimension=0,
        tiled=True,
    )
    owned = lax.psum_scatter(summed_rows, "occ", scatter_dimension=2, tiled=True)
    return -jnp.transpose(owned, (1, 0, 2))


VMEM = pl.BlockSpec(memory_space=pltpu.VMEM)
SMEM = pl.BlockSpec(memory_space=pltpu.SMEM)


def peer(position, hop, shards, back=False):
    if shards & (shards - 1) == 0:
        return position ^ hop
    moved = position + (shards - hop if back else hop)
    return moved % shards if isinstance(moved, int) else lax.rem(moved, shards)


def passed_on(shards):
    return shards - 2 if shards > 2 and shards & (shards - 1) == 0 else None


def groups_of(shards):
    hops = list(range(shards - 1, -1, -1))
    return [hops[: shards // 2], hops[shards // 2 :]]


def load_body(half, place, source, out, arrived):
    del place
    vectors, part = out.shape[0] // STREAMS, out.shape[1]
    copies = []
    for at in range(STREAMS):
        some = pl.ds(at * vectors, vectors)
        copies.append(pltpu.make_async_copy(source.at[some, pl.ds(half * part, part)], out.at[some], arrived.at[at]))
    for copy in copies:
        copy.start()
    for copy in copies:
        copy.wait()


def loaded(place, factors, half):
    vectors, width, orbitals = factors.shape
    return pl.pallas_call(
        functools.partial(load_body, half),
        in_specs=[SMEM, pl.BlockSpec(memory_space=pltpu.HBM)],
        out_specs=VMEM,
        out_shape=pltpu.VMEM((vectors, width // HALVES, orbitals), factors.dtype),
        scratch_shapes=[pltpu.SemaphoreType.DMA((STREAMS,))],
        compiler_params=LARGE,
    )(place, factors)


def amplitude_body(shards, low, high, place, factors, *refs):
    pieces, own, far, rows = refs[:-3], refs[-3], refs[-2], refs[-1]
    owned, width = pieces[0].shape[0], own.shape[1]
    for step in range(shards):
        at = pl.multiple_of(peer(place[0], step, shards, True) * owned, owned)
        if len(pieces) == shards:
            rows[pl.ds(at, owned), :] = pieces[step][...]
        else:
            rows[pl.ds(at, owned), :width] = pieces[step][...]
            rows[pl.ds(at, owned), width:] = pieces[shards + step][...]
    part = factors.shape[1]
    for first in range(low, high, BLOCK):
        taken = jnp.concatenate([factors[g] for g in range(first, min(first + BLOCK, high))], axis=0)
        sums = jnp.dot(taken, rows[...], preferred_element_type=jnp.float32).astype(jnp.bfloat16)
        at = (first - low) * part
        own[at : at + sums.shape[0], :] = sums[:, :width]
        far[at : at + sums.shape[0], :] = sums[:, width:]


def amplitudes_of(place, factors, pieces, vectors, width, shards):
    orbitals = factors.shape[2]
    count = (vectors[1] - vectors[0]) * factors.shape[1]
    return pl.pallas_call(
        functools.partial(amplitude_body, shards, *vectors),
        in_specs=[SMEM] + [VMEM] * (1 + len(pieces)),
        out_specs=[VMEM] * 2,
        scratch_shapes=[pltpu.VMEM((orbitals, 2 * width), jnp.bfloat16)],
        out_shape=[jax.ShapeDtypeStruct((count, width), jnp.bfloat16)] * 2,
        compiler_params=SMALL,
        cost_estimate=pl.CostEstimate(flops=4 * count * orbitals * width, transcendentals=0, bytes_accessed=2 * count * orbitals),
    )(place, factors, *pieces)


def gradient_body(shards, parts, first, carried, group, place, *refs):
    owns, fars, factors = refs[:parts], refs[parts : 2 * parts], refs[2 * parts : 2 * parts + HALVES]
    outs, sums = refs[2 * parts + HALVES + carried : -1], refs[-1]
    width = owns[0].shape[1]
    part = width // HALVES
    slots = [(at, g) for at, own in enumerate(owns) for g in range(own.shape[0] // part)]
    owned = factors[0].shape[2] // shards

    def wide(vectors):
        sides = [jnp.concatenate([side[at][g * part : (g + 1) * part, :] for at, g in vectors], axis=1) for side in (owns, fars)]
        return jnp.concatenate(sides, axis=0)

    def columns_of(hop):
        return pl.ds(pl.multiple_of(peer(place[0], hop, shards) * owned, owned), owned)

    if group is not None:
        taken = wide(slots)
        for at, hop in enumerate(group):
            columns = columns_of(hop)
            rows = jnp.concatenate([loaded[g, :, columns] for g in range(first, first + len(slots)) for loaded in factors], axis=0)
            total = refs[2 * parts + HALVES][:, columns] + jnp.dot(taken, rows, preferred_element_type=jnp.float32)
            outs[at][...] = total[:part]
            outs[-1][:, at * owned : (at + 1) * owned] = total[part:].astype(jnp.bfloat16)
        return

    for seen in range(0, len(slots), BLOCK):
        vectors = slots[seen : seen + BLOCK]
        low = first + seen
        rows = jnp.concatenate([loaded[g] for g in range(low, low + len(vectors)) for loaded in factors], axis=0)
        grown = jnp.dot(wide(vectors), rows, preferred_element_type=jnp.float32)
        if seen == 0:
            sums[...] = grown
        else:
            sums[...] += grown
    if len(outs) == 1:
        outs[0][...] = sums[...]
        return
    for hop in range(shards):
        outs[hop][...] = sums[:, columns_of(hop)].astype(outs[hop].dtype)


def gradients_of(place, factors, owns, fars, shards, first=0, group=None, carried=None, more=False):
    orbitals, width = factors[0].shape[2], owns[0].shape[1]
    part, owned = width // HALVES, orbitals // shards
    outs = [jax.ShapeDtypeStruct((2 * part, owned), jnp.bfloat16 if hop else jnp.float32) for hop in range(shards)]
    if more:
        outs = [jax.ShapeDtypeStruct((2 * part, orbitals), jnp.float32)]
    elif group:
        outs = [jax.ShapeDtypeStruct((part, owned), jnp.float32)] * len(group)
        outs += [jax.ShapeDtypeStruct((part, owned * len(group)), jnp.bfloat16)]
    count = sum(own.shape[0] for own in owns) * HALVES
    values = [place, *owns, *fars, *factors] + ([] if carried is None else [carried])
    return pl.pallas_call(
        functools.partial(gradient_body, shards, len(owns), first, 0 if carried is None else 1, group),
        in_specs=[SMEM] + [VMEM] * (len(values) - 1),
        out_specs=[VMEM] * len(outs),
        scratch_shapes=[pltpu.VMEM((2 * part, orbitals), jnp.float32)],
        out_shape=outs,
        compiler_params=SMALL,
        cost_estimate=pl.CostEstimate(flops=4 * count * orbitals * part, transcendentals=0, bytes_accessed=2 * count * orbitals),
    )(*values)


def split_body(each, *refs):
    inputs, outs = refs[: -(len(refs) // (each + 1)) - 1], refs[-(len(refs) // (each + 1)) - 1 :]
    for stage, own in enumerate(outs[:-1]):
        parts = inputs[stage * each : (stage + 1) * each]
        total = parts[0][...].astype(jnp.float32)
        for part in parts[1:]:
            total = total + part[...].astype(jnp.float32)
        half = own.shape[0]
        own[...] = total[:half]
        outs[-1][stage * half : (stage + 1) * half, :] = total[half:].astype(jnp.bfloat16)


def split_sums(stages):
    rows, columns = stages[0][0].shape
    outs = [jax.ShapeDtypeStruct((rows // 2, columns), jnp.float32)] * len(stages)
    outs += [jax.ShapeDtypeStruct((len(stages) * (rows // 2), columns), jnp.bfloat16)]
    flat = [part for stage in stages for part in stage]
    return pl.pallas_call(functools.partial(split_body, len(stages[0])), out_shape=outs, compiler_params=SMALL)(*flat)


def join_body(came, *refs):
    count = len(refs) // 2
    for at in range(count):
        own, out = refs[at], refs[count + at]
        columns = own.shape[1]
        out[...] = (own[...] + came[:, at * columns : (at + 1) * columns].astype(jnp.float32)).astype(out.dtype)


def join_sums(came, owns, kinds):
    outs = [jax.ShapeDtypeStruct(own.shape, kind) for own, kind in zip(owns, kinds)]
    return pl.pallas_call(join_body, out_shape=outs, compiler_params=SMALL)(came, *owns)


def total_body(plan, *refs):
    out = refs[-1]
    for walker, halves in enumerate(plan):

        @pl.when(pl.program_id(0) == walker)
        def add(halves=halves):
            rows = []
            for parts in halves:
                total = None
                for at, low, high in parts:
                    value = refs[at][low:high, :].astype(jnp.float32)
                    total = value if total is None else total + value
                rows.append(total)
            out[0] = -jnp.concatenate(rows, axis=0).T


def totals_of(values, plan):
    part, owned = values[0].shape
    return pl.pallas_call(
        functools.partial(total_body, plan),
        grid=(len(plan),),
        in_specs=[VMEM] * len(values),
        out_specs=pl.BlockSpec((1, owned, part * HALVES), lambda walker: (walker, 0, 0)),
        out_shape=jax.ShapeDtypeStruct((len(plan), owned, part * HALVES), jnp.float32),
        compiler_params=SMALL,
    )(*values)


def parts_of(stage, stages, vectors):
    if stage == 0:
        return [0, vectors // 4, vectors]
    if stage == stages - 1:
        return [0, vectors - vectors // 4, vectors]
    return [0, vectors]


def paired(shape, chol_half, theta):
    return in_order(shape, chol_half, theta)


def in_order(shape, chol_half, theta):
    shards = shape["vec"]
    vectors, width, _ = chol_half.shape
    walkers = theta.shape[0]
    position = lax.axis_index("vec")
    place = position.reshape(1)
    factors = []
    for half in range(HALVES):
        factors.append(loaded(place, chol_half, half))

    def flat(grp, vec, occ, wlk):
        return ((grp * shape["vec"] + vec) * shape["occ"] + occ) * shape["wlk"] + wlk

    def moved(value, hop, across=False):
        pairs = [
            (flat(grp, vec, occ, wlk), flat(grp, peer(vec, hop, shards), 1 - occ if across else occ, wlk))
            for grp in range(shape["grp"])
            for vec in range(shards)
            for occ in range(shape["occ"])
            for wlk in range(shape["wlk"])
        ]
        return lax.ppermute(value, AXES, pairs)

    hops = range(1, shards)
    near = [theta[0]] + [moved(theta[0], hop) for hop in hops]
    across = moved(theta, 0, True)
    blocks = [near + [across[0]] + [moved(near[hop], 0, True) for hop in hops]]
    for walker in range(1, walkers):
        both = jnp.concatenate([theta[walker], across[walker]], axis=1)
        pieces = {hop: moved(both, hop) for hop in hops if hop != passed_on(shards)}
        if passed_on(shards):
            pieces[passed_on(shards)] = moved(pieces[shards - 1], 1)
        blocks.append([both] + [pieces[hop] for hop in hops])

    stages = walkers * HALVES
    sides = []
    for stage in range(stages):
        owns, fars = [], []
        cuts = parts_of(stage, stages, vectors)
        for part in zip(cuts[:-1], cuts[1:]):
            own, far = amplitudes_of(place, factors[stage % HALVES], blocks[stage // HALVES], part, width, shards)
            owns.append(own)
            fars.append(moved(far, 0, True))
        sides.append((owns, fars))

    arrived = []
    for stage in range(stages - 1):
        got = gradients_of(place, factors, *sides[stage], shards)
        arrived.append([got[0]] + [moved(got[hop], hop) for hop in hops])
    *kept, crossing = split_sums(arrived)
    part = width // HALVES
    values = [*kept, moved(crossing, 0, True)]
    plan = [[(stage, 0, part), (len(kept), stage * part, (stage + 1) * part)] for stage in range(len(kept))]

    owns, fars = sides[-1]
    groups = groups_of(shards)
    (carried,) = gradients_of(place, factors, owns[:1], fars[:1], shards, more=True)
    cut = parts_of(stages - 1, stages, vectors)[1]
    ends = [None] * shards
    for group in groups:
        *own, far = gradients_of(place, factors, owns[1:], fars[1:], shards, cut, group, carried)
        came = moved(far, 0, True)
        joined = join_sums(came, own, [jnp.bfloat16 if hop else jnp.float32 for hop in group])
        for hop, value in zip(group, joined):
            ends[hop] = moved(value, hop) if hop else value
    plan.append([(len(values) + at, 0, part) for at in range(shards)])
    values += ends
    return totals_of(values, [plan[walker * HALVES : (walker + 1) * HALVES] for walker in range(walkers)])


def solution(mesh):
    placed = (P(("grp", "vec"), "occ", None), P(("grp", "wlk"), "vec", "occ"))
    pairs = mesh.shape["occ"] == 2
    return jax.shard_map(
        functools.partial(paired, dict(mesh.shape)) if pairs else general,
        mesh=mesh,
        in_specs=placed,
        out_specs=P(("grp", "wlk"), "vec", "occ"),
        check_vma=False,
    )
```

```python
import functools

import jax
import jax.numpy as jnp
from jax import lax
from jax.experimental import pallas as pl
from jax.experimental.pallas import tpu as pltpu
from jax.sharding import PartitionSpec as P


AXES = ("grp", "vec", "occ", "wlk")
HALVES = 2
STREAMS = 4
BLOCK = 8
LARGE = pltpu.CompilerParams(vmem_limit_bytes=44 * 2**20)
SMALL = pltpu.CompilerParams(vmem_limit_bytes=24 * 2**20)


def general(chol_half, theta):
    widened = lax.all_gather(theta, "occ", axis=2, tiled=True)
    amplitude_sums = jnp.einsum(
        "gip,wpj->wgij",
        chol_half,
        lax.all_gather(widened, "vec", axis=1, tiled=True),
        preferred_element_type=jnp.float32,
    )
    amplitudes = amplitude_sums.astype(jnp.bfloat16)
    swapped = lax.all_to_all(amplitudes, "occ", split_axis=3, concat_axis=2, tiled=True)
    summed_rows = lax.psum_scatter(
        jnp.einsum("gap,wgba->pwb", chol_half, swapped, preferred_element_type=jnp.float32),
        "vec",
        scatter_dimension=0,
        tiled=True,
    )
    owned = lax.psum_scatter(summed_rows, "occ", scatter_dimension=2, tiled=True)
    return -jnp.transpose(owned, (1, 0, 2))


VMEM = pl.BlockSpec(memory_space=pltpu.VMEM)
SMEM = pl.BlockSpec(memory_space=pltpu.SMEM)


def peer(position, hop, shards, back=False):
    if shards & (shards - 1) == 0:
        return position ^ hop
    moved = position + (shards - hop if back else hop)
    return moved % shards if isinstance(moved, int) else lax.rem(moved, shards)


def hops_of(shards):
    return sorted(range(1, shards), key=lambda hop: (hop != shards - 1, hop))


def passed_on(shards):
    return shards - 2 if shards > 2 and shards & (shards - 1) == 0 else None


def groups_of(shards):
    hops = hops_of(shards) + [0]
    return [hops[: shards // 2], hops[shards // 2 :]]


def load_body(half, place, source, out, arrived):
    del place
    vectors, part = out.shape[0] // STREAMS, out.shape[1]
    copies = []
    for at in range(STREAMS):
        some = pl.ds(at * vectors, vectors)
        copies.append(pltpu.make_async_copy(source.at[some, pl.ds(half * part, part)], out.at[some], arrived.at[at]))
    for copy in copies:
        copy.start()
    for copy in copies:
        copy.wait()


def loaded(place, factors, half):
    vectors, width, orbitals = factors.shape
    return pl.pallas_call(
        functools.partial(load_body, half),
        in_specs=[SMEM, pl.BlockSpec(memory_space=pltpu.HBM)],
        out_specs=VMEM,
        out_shape=pltpu.VMEM((vectors, width // HALVES, orbitals), factors.dtype),
        scratch_shapes=[pltpu.SemaphoreType.DMA((STREAMS,))],
        compiler_params=LARGE,
    )(place, factors)


def amplitude_body(shards, low, high, place, factors, *refs):
    pieces, own, far, rows = refs[:-3], refs[-3], refs[-2], refs[-1]
    owned, width = pieces[0].shape[0], own.shape[1]
    for step in range(shards):
        at = pl.multiple_of(peer(place[0], step, shards, True) * owned, owned)
        if len(pieces) == shards:
            rows[pl.ds(at, owned), :] = pieces[step][...]
        else:
            rows[pl.ds(at, owned), :width] = pieces[step][...]
            rows[pl.ds(at, owned), width:] = pieces[shards + step][...]
    part = factors.shape[1]
    for first in range(low, high, BLOCK):
        taken = jnp.concatenate([factors[g] for g in range(first, min(first + BLOCK, high))], axis=0)
        sums = jnp.dot(taken, rows[...], preferred_element_type=jnp.float32).astype(jnp.bfloat16)
        at = (first - low) * part
        own[at : at + sums.shape[0], :] = sums[:, :width]
        far[at : at + sums.shape[0], :] = sums[:, width:]


def amplitudes_of(place, factors, pieces, vectors, width, shards):
    orbitals = factors.shape[2]
    count = (vectors[1] - vectors[0]) * factors.shape[1]
    return pl.pallas_call(
        functools.partial(amplitude_body, shards, *vectors),
        in_specs=[SMEM] + [VMEM] * (1 + len(pieces)),
        out_specs=[VMEM] * 2,
        scratch_shapes=[pltpu.VMEM((orbitals, 2 * width), jnp.bfloat16)],
        out_shape=[jax.ShapeDtypeStruct((count, width), jnp.bfloat16)] * 2,
        compiler_params=SMALL,
        cost_estimate=pl.CostEstimate(flops=4 * count * orbitals * width, transcendentals=0, bytes_accessed=2 * count * orbitals),
    )(place, factors, *pieces)


def gradient_body(shards, parts, first, carried, group, place, *refs):
    owns, fars, factors = refs[:parts], refs[parts : 2 * parts], refs[2 * parts : 2 * parts + HALVES]
    outs, sums = refs[2 * parts + HALVES + carried : -1], refs[-1]
    width = owns[0].shape[1]
    part = width // HALVES
    slots = [(at, g) for at, own in enumerate(owns) for g in range(own.shape[0] // part)]
    owned = factors[0].shape[2] // shards

    def wide(vectors):
        sides = [jnp.concatenate([side[at][g * part : (g + 1) * part, :] for at, g in vectors], axis=1) for side in (owns, fars)]
        return jnp.concatenate(sides, axis=0)

    def columns_of(hop):
        return pl.ds(pl.multiple_of(peer(place[0], hop, shards) * owned, owned), owned)

    if group is not None:
        taken = wide(slots)
        for at, hop in enumerate(group):
            columns = columns_of(hop)
            rows = jnp.concatenate([loaded[g, :, columns] for g in range(first, first + len(slots)) for loaded in factors], axis=0)
            total = refs[2 * parts + HALVES][:, columns] + jnp.dot(taken, rows, preferred_element_type=jnp.float32)
            outs[at][...] = total[:part]
            outs[-1][:, at * owned : (at + 1) * owned] = total[part:].astype(jnp.bfloat16)
        return

    for seen in range(0, len(slots), BLOCK):
        vectors = slots[seen : seen + BLOCK]
        low = first + seen
        rows = jnp.concatenate([loaded[g] for g in range(low, low + len(vectors)) for loaded in factors], axis=0)
        grown = jnp.dot(wide(vectors), rows, preferred_element_type=jnp.float32)
        if seen == 0:
            sums[...] = grown
        else:
            sums[...] += grown
    if len(outs) == 1:
        outs[0][...] = sums[...]
        return
    for hop in range(shards):
        outs[hop][...] = sums[:, columns_of(hop)].astype(outs[hop].dtype)


def gradients_of(place, factors, owns, fars, shards, first=0, group=None, carried=None, more=False):
    orbitals, width = factors[0].shape[2], owns[0].shape[1]
    part, owned = width // HALVES, orbitals // shards
    outs = [jax.ShapeDtypeStruct((2 * part, owned), jnp.bfloat16 if hop else jnp.float32) for hop in range(shards)]
    if more:
        outs = [jax.ShapeDtypeStruct((2 * part, orbitals), jnp.float32)]
    elif group:
        outs = [jax.ShapeDtypeStruct((part, owned), jnp.float32)] * len(group)
        outs += [jax.ShapeDtypeStruct((part, owned * len(group)), jnp.bfloat16)]
    count = sum(own.shape[0] for own in owns) * HALVES
    values = [place, *owns, *fars, *factors] + ([] if carried is None else [carried])
    return pl.pallas_call(
        functools.partial(gradient_body, shards, len(owns), first, 0 if carried is None else 1, group),
        in_specs=[SMEM] + [VMEM] * (len(values) - 1),
        out_specs=[VMEM] * len(outs),
        scratch_shapes=[pltpu.VMEM((2 * part, orbitals), jnp.float32)],
        out_shape=outs,
        compiler_params=SMALL,
        cost_estimate=pl.CostEstimate(flops=4 * count * orbitals * part, transcendentals=0, bytes_accessed=2 * count * orbitals),
    )(*values)


def split_body(each, *refs):
    inputs, outs = refs[: -(len(refs) // (each + 1)) - 1], refs[-(len(refs) // (each + 1)) - 1 :]
    for stage, own in enumerate(outs[:-1]):
        parts = inputs[stage * each : (stage + 1) * each]
        total = parts[0][...].astype(jnp.float32)
        for part in parts[1:]:
            total = total + part[...].astype(jnp.float32)
        half = own.shape[0]
        own[...] = total[:half]
        outs[-1][stage * half : (stage + 1) * half, :] = total[half:].astype(jnp.bfloat16)


def split_sums(stages):
    rows, columns = stages[0][0].shape
    outs = [jax.ShapeDtypeStruct((rows // 2, columns), jnp.float32)] * len(stages)
    outs += [jax.ShapeDtypeStruct((len(stages) * (rows // 2), columns), jnp.bfloat16)]
    flat = [part for stage in stages for part in stage]
    return pl.pallas_call(functools.partial(split_body, len(stages[0])), out_shape=outs, compiler_params=SMALL)(*flat)


def join_body(came, *refs):
    count = len(refs) // 2
    for at in range(count):
        own, out = refs[at], refs[count + at]
        columns = own.shape[1]
        out[...] = (own[...] + came[:, at * columns : (at + 1) * columns].astype(jnp.float32)).astype(out.dtype)


def join_sums(came, owns, kinds):
    outs = [jax.ShapeDtypeStruct(own.shape, kind) for own, kind in zip(owns, kinds)]
    return pl.pallas_call(join_body, out_shape=outs, compiler_params=SMALL)(came, *owns)


def total_body(plan, *refs):
    rows = []
    for parts in plan:
        total = None
        for at, low, high in parts:
            value = refs[at][low:high, :].astype(jnp.float32)
            total = value if total is None else total + value
        rows.append(total)
    refs[-1][0] = -jnp.concatenate(rows, axis=0).T


def total_of(values, plan, walker, walkers, before):
    part, owned = values[0].shape
    used = sorted({at for parts in plan for at, low, high in parts})
    plan = [[(used.index(at), low, high) for at, low, high in parts] for parts in plan]
    taken = [values[at] for at in used]
    return pl.pallas_call(
        functools.partial(total_body, plan),
        grid=(1,),
        in_specs=[VMEM] * len(taken) + ([] if before is None else [pl.BlockSpec(memory_space=pltpu.HBM)]),
        out_specs=pl.BlockSpec((1, owned, part * HALVES), lambda i: (walker, 0, 0)),
        out_shape=jax.ShapeDtypeStruct((walkers, owned, part * HALVES), jnp.float32),
        input_output_aliases={} if before is None else {len(taken): 0},
        compiler_params=SMALL,
    )(*taken, *([] if before is None else [before]))


def parts_of(stage, stages, vectors):
    if stage == 0:
        return [0, vectors // 4, vectors]
    if stage == stages - 1:
        return [0, vectors - vectors // 4, vectors]
    return [0, vectors]


def paired(shape, chol_half, theta):
    return in_order(shape, chol_half, theta)


def in_order(shape, chol_half, theta):
    shards = shape["vec"]
    vectors, width, _ = chol_half.shape
    walkers = theta.shape[0]
    position = lax.axis_index("vec")
    place = position.reshape(1)
    factors = []
    for half in range(HALVES):
        factors.append(loaded(place, chol_half, half))

    def flat(grp, vec, occ, wlk):
        return ((grp * shape["vec"] + vec) * shape["occ"] + occ) * shape["wlk"] + wlk

    def moved(value, hop, across=False):
        pairs = [
            (flat(grp, vec, occ, wlk), flat(grp, peer(vec, hop, shards), 1 - occ if across else occ, wlk))
            for grp in range(shape["grp"])
            for vec in range(shards)
            for occ in range(shape["occ"])
            for wlk in range(shape["wlk"])
        ]
        return lax.ppermute(value, AXES, pairs)

    hops = range(1, shards)
    near = [theta[0]] + [moved(theta[0], hop) for hop in hops]
    across = moved(theta, 0, True)
    blocks = [near + [across[0]] + [moved(near[hop], 0, True) for hop in hops]]
    for walker in range(1, walkers):
        both = jnp.concatenate([theta[walker], across[walker]], axis=1)
        pieces = {hop: moved(both, hop) for hop in hops if hop != passed_on(shards)}
        if passed_on(shards):
            pieces[passed_on(shards)] = moved(pieces[shards - 1], 1)
        blocks.append([both] + [pieces[hop] for hop in hops])

    stages = walkers * HALVES
    sides = []
    for stage in range(stages):
        owns, fars = [], []
        cuts = parts_of(stage, stages, vectors)
        for part in zip(cuts[:-1], cuts[1:]):
            own, far = amplitudes_of(place, factors[stage % HALVES], blocks[stage // HALVES], part, width, shards)
            owns.append(own)
            fars.append(moved(far, 0, True))
        sides.append((owns, fars))

    arrived = []
    for stage in range(stages - 1):
        got = gradients_of(place, factors, *sides[stage], shards)
        arrived.append([got[0]] + [moved(got[hop], hop) for hop in hops])
    part, values, plan = width // HALVES, [], []
    for some in (arrived[: stages - HALVES], arrived[stages - HALVES :]):
        *kept, crossing = split_sums(some)
        here = len(values)
        values += [*kept, moved(crossing, 0, True)]
        plan += [[(here + stage, 0, part), (here + len(kept), stage * part, (stage + 1) * part)] for stage in range(len(kept))]

    owns, fars = sides[-1]
    groups = groups_of(shards)
    (carried,) = gradients_of(place, factors, owns[:1], fars[:1], shards, more=True)
    cut = parts_of(stages - 1, stages, vectors)[1]
    ends = [None] * shards
    for group in groups:
        *own, far = gradients_of(place, factors, owns[1:], fars[1:], shards, cut, group, carried)
        came = moved(far, 0, True)
        joined = join_sums(came, own, [jnp.bfloat16 if hop else jnp.float32 for hop in group])
        for hop, value in zip(group, joined):
            ends[hop] = moved(value, hop) if hop else value
    plan.append([(len(values) + at, 0, part) for at in range(shards)])
    values += ends
    total = None
    for walker in range(walkers):
        total = total_of(values, plan[walker * HALVES : (walker + 1) * HALVES], walker, walkers, total)
    return total


def solution(mesh):
    placed = (P(("grp", "vec"), "occ", None), P(("grp", "wlk"), "vec", "occ"))
    pairs = mesh.shape["occ"] == 2
    return jax.shard_map(
        functools.partial(paired, dict(mesh.shape)) if pairs else general,
        mesh=mesh,
        in_specs=placed,
        out_specs=P(("grp", "wlk"), "vec", "occ"),
        check_vma=False,
    )
```

```python
import functools

import jax
import jax.numpy as jnp
from jax import lax
from jax.experimental import pallas as pl
from jax.experimental.pallas import tpu as pltpu
from jax.sharding import PartitionSpec as P


AXES = ("grp", "vec", "occ", "wlk")
HALVES = 2
STREAMS = 4
BLOCK = 8
LARGE = pltpu.CompilerParams(vmem_limit_bytes=44 * 2**20)
SMALL = pltpu.CompilerParams(vmem_limit_bytes=24 * 2**20)


def general(chol_half, theta):
    widened = lax.all_gather(theta, "occ", axis=2, tiled=True)
    amplitude_sums = jnp.einsum(
        "gip,wpj->wgij",
        chol_half,
        lax.all_gather(widened, "vec", axis=1, tiled=True),
        preferred_element_type=jnp.float32,
    )
    amplitudes = amplitude_sums.astype(jnp.bfloat16)
    swapped = lax.all_to_all(amplitudes, "occ", split_axis=3, concat_axis=2, tiled=True)
    summed_rows = lax.psum_scatter(
        jnp.einsum("gap,wgba->pwb", chol_half, swapped, preferred_element_type=jnp.float32),
        "vec",
        scatter_dimension=0,
        tiled=True,
    )
    owned = lax.psum_scatter(summed_rows, "occ", scatter_dimension=2, tiled=True)
    return -jnp.transpose(owned, (1, 0, 2))


VMEM = pl.BlockSpec(memory_space=pltpu.VMEM)
SMEM = pl.BlockSpec(memory_space=pltpu.SMEM)


def peer(position, hop, shards, back=False):
    if shards & (shards - 1) == 0:
        return position ^ hop
    moved = position + (shards - hop if back else hop)
    return moved % shards if isinstance(moved, int) else lax.rem(moved, shards)


def passed_on(shards):
    return shards - 2 if shards > 2 and shards & (shards - 1) == 0 else None


def load_body(half, place, source, out, arrived):
    del place
    vectors, part = out.shape[0] // STREAMS, out.shape[1]
    copies = []
    for at in range(STREAMS):
        some = pl.ds(at * vectors, vectors)
        copies.append(pltpu.make_async_copy(source.at[some, pl.ds(half * part, part)], out.at[some], arrived.at[at]))
    for copy in copies:
        copy.start()
    for copy in copies:
        copy.wait()


def loaded(place, factors, half):
    vectors, width, orbitals = factors.shape
    return pl.pallas_call(
        functools.partial(load_body, half),
        in_specs=[SMEM, pl.BlockSpec(memory_space=pltpu.HBM)],
        out_specs=VMEM,
        out_shape=pltpu.VMEM((vectors, width // HALVES, orbitals), factors.dtype),
        scratch_shapes=[pltpu.SemaphoreType.DMA((STREAMS,))],
        compiler_params=LARGE,
    )(place, factors)


def amplitude_body(shards, low, high, place, factors, *refs):
    pieces, own, far, rows = refs[:-3], refs[-3], refs[-2], refs[-1]
    owned, width = pieces[0].shape[0], own.shape[1]
    for step in range(shards):
        at = pl.multiple_of(peer(place[0], step, shards, True) * owned, owned)
        if len(pieces) == shards:
            rows[pl.ds(at, owned), :] = pieces[step][...]
        else:
            rows[pl.ds(at, owned), :width] = pieces[step][...]
            rows[pl.ds(at, owned), width:] = pieces[shards + step][...]
    part = factors.shape[1]
    for first in range(low, high, BLOCK):
        taken = jnp.concatenate([factors[g] for g in range(first, min(first + BLOCK, high))], axis=0)
        sums = jnp.dot(taken, rows[...], preferred_element_type=jnp.float32).astype(jnp.bfloat16)
        at = (first - low) * part
        own[at : at + sums.shape[0], :] = sums[:, :width]
        far[at : at + sums.shape[0], :] = sums[:, width:]


def amplitudes_of(place, factors, pieces, vectors, width, shards):
    orbitals = factors.shape[2]
    count = (vectors[1] - vectors[0]) * factors.shape[1]
    return pl.pallas_call(
        functools.partial(amplitude_body, shards, *vectors),
        in_specs=[SMEM] + [VMEM] * (1 + len(pieces)),
        out_specs=[VMEM] * 2,
        scratch_shapes=[pltpu.VMEM((orbitals, 2 * width), jnp.bfloat16)],
        out_shape=[jax.ShapeDtypeStruct((count, width), jnp.bfloat16)] * 2,
        compiler_params=SMALL,
        cost_estimate=pl.CostEstimate(flops=4 * count * orbitals * width, transcendentals=0, bytes_accessed=2 * count * orbitals),
    )(place, factors, *pieces)


def gradient_body(shards, parts, first, carried, apart, place, *refs):
    owns, fars, factors = refs[:parts], refs[parts : 2 * parts], refs[2 * parts : 2 * parts + HALVES]
    outs, sums = refs[2 * parts + HALVES + carried : -1], refs[-1]
    width = owns[0].shape[1]
    part = width // HALVES
    slots = [(at, g) for at, own in enumerate(owns) for g in range(own.shape[0] // part)]
    owned = factors[0].shape[2] // shards

    def wide(vectors):
        sides = [jnp.concatenate([side[at][g * part : (g + 1) * part, :] for at, g in vectors], axis=1) for side in (owns, fars)]
        return jnp.concatenate(sides, axis=0)

    def columns_of(hop):
        return pl.ds(pl.multiple_of(peer(place[0], hop, shards) * owned, owned), owned)

    for seen in range(0, len(slots), BLOCK):
        vectors = slots[seen : seen + BLOCK]
        low = first + seen
        rows = jnp.concatenate([loaded[g] for g in range(low, low + len(vectors)) for loaded in factors], axis=0)
        grown = jnp.dot(wide(vectors), rows, preferred_element_type=jnp.float32)
        if seen == 0 and carried:
            sums[...] = refs[2 * parts + HALVES][...] + grown
        elif seen == 0:
            sums[...] = grown
        else:
            sums[...] += grown
    if len(outs) == 1:
        outs[0][...] = sums[...]
        return
    for hop in range(shards):
        if apart:
            outs[hop][...] = sums[:part, columns_of(hop)].astype(outs[hop].dtype)
            outs[shards + hop][...] = sums[part:, columns_of(hop)].astype(outs[shards + hop].dtype)
        else:
            outs[hop][...] = sums[:, columns_of(hop)].astype(outs[hop].dtype)


def gradients_of(place, factors, owns, fars, shards, first=0, apart=False, carried=None, more=False):
    orbitals, width = factors[0].shape[2], owns[0].shape[1]
    part, owned = width // HALVES, orbitals // shards
    outs = [jax.ShapeDtypeStruct((2 * part, owned), jnp.bfloat16 if hop else jnp.float32) for hop in range(shards)]
    if more:
        outs = [jax.ShapeDtypeStruct((2 * part, orbitals), jnp.float32)]
    elif apart:
        outs = [jax.ShapeDtypeStruct((part, owned), jnp.bfloat16 if at else jnp.float32) for at in range(2 * shards)]
    count = sum(own.shape[0] for own in owns) * HALVES
    values = [place, *owns, *fars, *factors] + ([] if carried is None else [carried])
    return pl.pallas_call(
        functools.partial(gradient_body, shards, len(owns), first, 0 if carried is None else 1, apart),
        in_specs=[SMEM] + [VMEM] * (len(values) - 1),
        out_specs=[VMEM] * len(outs),
        scratch_shapes=[pltpu.VMEM((2 * part, orbitals), jnp.float32)],
        out_shape=outs,
        compiler_params=SMALL,
        cost_estimate=pl.CostEstimate(flops=4 * count * orbitals * part, transcendentals=0, bytes_accessed=2 * count * orbitals),
    )(*values)


def split_body(each, *refs):
    inputs, outs = refs[: -(len(refs) // (each + 1)) - 1], refs[-(len(refs) // (each + 1)) - 1 :]
    for stage, own in enumerate(outs[:-1]):
        parts = inputs[stage * each : (stage + 1) * each]
        total = parts[0][...].astype(jnp.float32)
        for part in parts[1:]:
            total = total + part[...].astype(jnp.float32)
        half = own.shape[0]
        own[...] = total[:half]
        outs[-1][stage * half : (stage + 1) * half, :] = total[half:].astype(jnp.bfloat16)


def split_sums(stages):
    rows, columns = stages[0][0].shape
    outs = [jax.ShapeDtypeStruct((rows // 2, columns), jnp.float32)] * len(stages)
    outs += [jax.ShapeDtypeStruct((len(stages) * (rows // 2), columns), jnp.bfloat16)]
    flat = [part for stage in stages for part in stage]
    return pl.pallas_call(functools.partial(split_body, len(stages[0])), out_shape=outs, compiler_params=SMALL)(*flat)


def total_body(plan, *refs):
    out = refs[-1]
    for walker, halves in enumerate(plan):

        @pl.when(pl.program_id(0) == walker)
        def add(halves=halves):
            rows = []
            for parts in halves:
                total = None
                for at, low, high in parts:
                    value = refs[at][low:high, :].astype(jnp.float32)
                    total = value if total is None else total + value
                rows.append(total)
            out[0] = -jnp.concatenate(rows, axis=0).T


def totals_of(values, plan):
    part, owned = values[0].shape
    return pl.pallas_call(
        functools.partial(total_body, plan),
        grid=(len(plan),),
        in_specs=[VMEM] * len(values),
        out_specs=pl.BlockSpec((1, owned, part * HALVES), lambda walker: (walker, 0, 0)),
        out_shape=jax.ShapeDtypeStruct((len(plan), owned, part * HALVES), jnp.float32),
        compiler_params=SMALL,
    )(*values)


def parts_of(stage, stages, vectors):
    if stage == 0:
        return [0, vectors // 4, vectors]
    if stage == stages - 1:
        return [0, vectors - vectors // 4, vectors]
    return [0, vectors]


def paired(shape, chol_half, theta):
    return in_order(shape, chol_half, theta)


def in_order(shape, chol_half, theta):
    shards = shape["vec"]
    vectors, width, _ = chol_half.shape
    walkers = theta.shape[0]
    position = lax.axis_index("vec")
    place = position.reshape(1)
    factors = []
    for half in range(HALVES):
        factors.append(loaded(place, chol_half, half))

    def flat(grp, vec, occ, wlk):
        return ((grp * shape["vec"] + vec) * shape["occ"] + occ) * shape["wlk"] + wlk

    def moved(value, hop, across=False):
        pairs = [
            (flat(grp, vec, occ, wlk), flat(grp, peer(vec, hop, shards), 1 - occ if across else occ, wlk))
            for grp in range(shape["grp"])
            for vec in range(shards)
            for occ in range(shape["occ"])
            for wlk in range(shape["wlk"])
        ]
        return lax.ppermute(value, AXES, pairs)

    hops = range(1, shards)
    near = [theta[0]] + [moved(theta[0], hop) for hop in hops]
    across = moved(theta, 0, True)
    blocks = [near + [across[0]] + [moved(near[hop], 0, True) for hop in hops]]
    for walker in range(1, walkers):
        both = jnp.concatenate([theta[walker], across[walker]], axis=1)
        pieces = {hop: moved(both, hop) for hop in hops if hop != passed_on(shards)}
        if passed_on(shards):
            pieces[passed_on(shards)] = moved(pieces[shards - 1], 1)
        blocks.append([both] + [pieces[hop] for hop in hops])

    stages = walkers * HALVES
    sides = []
    for stage in range(stages):
        owns, fars = [], []
        cuts = parts_of(stage, stages, vectors)
        for part in zip(cuts[:-1], cuts[1:]):
            own, far = amplitudes_of(place, factors[stage % HALVES], blocks[stage // HALVES], part, width, shards)
            owns.append(own)
            fars.append(moved(far, 0, True))
        sides.append((owns, fars))

    arrived = []
    for stage in range(stages - 1):
        got = gradients_of(place, factors, *sides[stage], shards)
        arrived.append([got[0]] + [moved(got[hop], hop) for hop in hops])
    *kept, crossing = split_sums(arrived)
    part = width // HALVES
    values = [*kept, moved(crossing, 0, True)]
    plan = [[(stage, 0, part), (len(kept), stage * part, (stage + 1) * part)] for stage in range(len(kept))]

    owns, fars = sides[-1]
    (carried,) = gradients_of(place, factors, owns[:1], fars[:1], shards, more=True)
    got = gradients_of(place, factors, owns[1:], fars[1:], shards, parts_of(stages - 1, stages, vectors)[1], True, carried)
    ends = [got[0]] + [moved(got[hop], hop) for hop in hops]
    ends += [moved(got[shards + hop], hop, True) for hop in range(shards)]
    plan.append([(len(values) + at, 0, part) for at in range(len(ends))])
    values += ends
    return totals_of(values, [plan[walker * HALVES : (walker + 1) * HALVES] for walker in range(walkers)])


def solution(mesh):
    placed = (P(("grp", "vec"), "occ", None), P(("grp", "wlk"), "vec", "occ"))
    pairs = mesh.shape["occ"] == 2
    return jax.shard_map(
        functools.partial(paired, dict(mesh.shape)) if pairs else general,
        mesh=mesh,
        in_specs=placed,
        out_specs=P(("grp", "wlk"), "vec", "occ"),
        check_vma=False,
    )
```

```python
import functools

import jax
import jax.numpy as jnp
from jax import lax
from jax.experimental import pallas as pl
from jax.experimental.pallas import tpu as pltpu
from jax.sharding import PartitionSpec as P


AXES = ("grp", "vec", "occ", "wlk")
HALVES = 2
STREAMS = 4
BLOCK = 8
LARGE = pltpu.CompilerParams(vmem_limit_bytes=44 * 2**20)
SMALL = pltpu.CompilerParams(vmem_limit_bytes=24 * 2**20)


def general(chol_half, theta):
    widened = lax.all_gather(theta, "occ", axis=2, tiled=True)
    amplitude_sums = jnp.einsum(
        "gip,wpj->wgij",
        chol_half,
        lax.all_gather(widened, "vec", axis=1, tiled=True),
        preferred_element_type=jnp.float32,
    )
    amplitudes = amplitude_sums.astype(jnp.bfloat16)
    swapped = lax.all_to_all(amplitudes, "occ", split_axis=3, concat_axis=2, tiled=True)
    summed_rows = lax.psum_scatter(
        jnp.einsum("gap,wgba->pwb", chol_half, swapped, preferred_element_type=jnp.float32),
        "vec",
        scatter_dimension=0,
        tiled=True,
    )
    owned = lax.psum_scatter(summed_rows, "occ", scatter_dimension=2, tiled=True)
    return -jnp.transpose(owned, (1, 0, 2))


VMEM = pl.BlockSpec(memory_space=pltpu.VMEM)
SMEM = pl.BlockSpec(memory_space=pltpu.SMEM)


def peer(position, hop, shards, back=False):
    if shards & (shards - 1) == 0:
        return position ^ hop
    moved = position + (shards - hop if back else hop)
    return moved % shards if isinstance(moved, int) else lax.rem(moved, shards)


def passed_on(shards):
    return shards - 2 if shards > 2 and shards & (shards - 1) == 0 else None


def groups_of(shards):
    hops = list(range(shards - 1, -1, -1))
    return [hops[: shards // 2], hops[shards // 2 :]]


def load_body(half, place, source, out, arrived):
    del place
    vectors, part = out.shape[:2]
    cuts = [vectors * at // STREAMS for at in range(STREAMS + 1)]
    copies = []
    for at, (low, high) in enumerate(zip(cuts[:-1], cuts[1:])):
        some = pl.ds(low, high - low)
        copies.append(pltpu.make_async_copy(source.at[some, pl.ds(half * part, part)], out.at[some], arrived.at[at]))
    for copy in copies:
        copy.start()
    for copy in copies:
        copy.wait()


def loaded(place, factors, half):
    vectors, width, orbitals = factors.shape
    return pl.pallas_call(
        functools.partial(load_body, half),
        in_specs=[SMEM, pl.BlockSpec(memory_space=pltpu.HBM)],
        out_specs=VMEM,
        out_shape=pltpu.VMEM((vectors, width // HALVES, orbitals), factors.dtype),
        scratch_shapes=[pltpu.SemaphoreType.DMA((STREAMS,))],
        compiler_params=LARGE,
    )(place, factors)


def amplitude_body(shards, low, high, place, factors, *refs):
    pieces, own, far, rows = refs[:-3], refs[-3], refs[-2], refs[-1]
    owned, width = pieces[0].shape[0], own.shape[1]
    for step in range(shards):
        at = pl.multiple_of(peer(place[0], step, shards, True) * owned, owned)
        if len(pieces) == shards:
            rows[pl.ds(at, owned), :] = pieces[step][...]
        else:
            rows[pl.ds(at, owned), :width] = pieces[step][...]
            rows[pl.ds(at, owned), width:] = pieces[shards + step][...]
    part = factors.shape[1]
    for first in range(low, high, BLOCK):
        taken = jnp.concatenate([factors[g] for g in range(first, min(first + BLOCK, high))], axis=0)
        sums = jnp.dot(taken, rows[...], preferred_element_type=jnp.float32).astype(jnp.bfloat16)
        at = (first - low) * part
        own[at : at + sums.shape[0], :] = sums[:, :width]
        far[at : at + sums.shape[0], :] = sums[:, width:]


def amplitudes_of(place, factors, pieces, vectors, width, shards):
    orbitals = factors.shape[2]
    count = (vectors[1] - vectors[0]) * factors.shape[1]
    return pl.pallas_call(
        functools.partial(amplitude_body, shards, *vectors),
        in_specs=[SMEM] + [VMEM] * (1 + len(pieces)),
        out_specs=[VMEM] * 2,
        scratch_shapes=[pltpu.VMEM((orbitals, 2 * width), jnp.bfloat16)],
        out_shape=[jax.ShapeDtypeStruct((count, width), jnp.bfloat16)] * 2,
        compiler_params=SMALL,
        cost_estimate=pl.CostEstimate(flops=4 * count * orbitals * width, transcendentals=0, bytes_accessed=2 * count * orbitals),
    )(place, factors, *pieces)


def gradient_body(shards, parts, first, carried, group, place, *refs):
    owns, fars, factors = refs[:parts], refs[parts : 2 * parts], refs[2 * parts : 2 * parts + HALVES]
    outs, sums = refs[2 * parts + HALVES + carried : -1], refs[-1]
    width = owns[0].shape[1]
    part = width // HALVES
    slots = [(at, g) for at, own in enumerate(owns) for g in range(own.shape[0] // part)]
    owned = factors[0].shape[2] // shards

    def wide(vectors):
        sides = [jnp.concatenate([side[at][g * part : (g + 1) * part, :] for at, g in vectors], axis=1) for side in (owns, fars)]
        return jnp.concatenate(sides, axis=0)

    def columns_of(hop):
        return pl.ds(pl.multiple_of(peer(place[0], hop, shards) * owned, owned), owned)

    if group is not None:
        taken = wide(slots)
        for at, hop in enumerate(group):
            columns = columns_of(hop)
            rows = jnp.concatenate([loaded[g, :, columns] for g in range(first, first + len(slots)) for loaded in factors], axis=0)
            total = refs[2 * parts + HALVES][:, columns] + jnp.dot(taken, rows, preferred_element_type=jnp.float32)
            outs[at][...] = total[:part]
            outs[-1][:, at * owned : (at + 1) * owned] = total[part:].astype(jnp.bfloat16)
        return

    for seen in range(0, len(slots), BLOCK):
        vectors = slots[seen : seen + BLOCK]
        low = first + seen
        rows = jnp.concatenate([loaded[g] for g in range(low, low + len(vectors)) for loaded in factors], axis=0)
        grown = jnp.dot(wide(vectors), rows, preferred_element_type=jnp.float32)
        if seen == 0:
            sums[...] = grown
        else:
            sums[...] += grown
    if len(outs) == 1:
        outs[0][...] = sums[...]
        return
    for hop in range(shards):
        outs[hop][...] = sums[:, columns_of(hop)].astype(outs[hop].dtype)


def gradients_of(place, factors, owns, fars, shards, first=0, group=None, carried=None, more=False):
    orbitals, width = factors[0].shape[2], owns[0].shape[1]
    part, owned = width // HALVES, orbitals // shards
    outs = [jax.ShapeDtypeStruct((2 * part, owned), jnp.bfloat16 if hop else jnp.float32) for hop in range(shards)]
    if more:
        outs = [jax.ShapeDtypeStruct((2 * part, orbitals), jnp.float32)]
    elif group:
        outs = [jax.ShapeDtypeStruct((part, owned), jnp.float32)] * len(group)
        outs += [jax.ShapeDtypeStruct((part, owned * len(group)), jnp.bfloat16)]
    count = sum(own.shape[0] for own in owns) * HALVES
    values = [place, *owns, *fars, *factors] + ([] if carried is None else [carried])
    return pl.pallas_call(
        functools.partial(gradient_body, shards, len(owns), first, 0 if carried is None else 1, group),
        in_specs=[SMEM] + [VMEM] * (len(values) - 1),
        out_specs=[VMEM] * len(outs),
        scratch_shapes=[pltpu.VMEM((2 * part, orbitals), jnp.float32)],
        out_shape=outs,
        compiler_params=SMALL,
        cost_estimate=pl.CostEstimate(flops=4 * count * orbitals * part, transcendentals=0, bytes_accessed=2 * count * orbitals),
    )(*values)


def split_body(each, *refs):
    inputs, outs = refs[: -(len(refs) // (each + 1)) - 1], refs[-(len(refs) // (each + 1)) - 1 :]
    for stage, own in enumerate(outs[:-1]):
        parts = inputs[stage * each : (stage + 1) * each]
        total = parts[0][...].astype(jnp.float32)
        for part in parts[1:]:
            total = total + part[...].astype(jnp.float32)
        half = own.shape[0]
        own[...] = total[:half]
        outs[-1][stage * half : (stage + 1) * half, :] = total[half:].astype(jnp.bfloat16)


def split_sums(stages):
    rows, columns = stages[0][0].shape
    outs = [jax.ShapeDtypeStruct((rows // 2, columns), jnp.float32)] * len(stages)
    outs += [jax.ShapeDtypeStruct((len(stages) * (rows // 2), columns), jnp.bfloat16)]
    flat = [part for stage in stages for part in stage]
    return pl.pallas_call(functools.partial(split_body, len(stages[0])), out_shape=outs, compiler_params=SMALL)(*flat)


def join_body(came, *refs):
    count = len(refs) // 2
    for at in range(count):
        own, out = refs[at], refs[count + at]
        columns = own.shape[1]
        out[...] = (own[...] + came[:, at * columns : (at + 1) * columns].astype(jnp.float32)).astype(out.dtype)


def join_sums(came, owns, kinds):
    outs = [jax.ShapeDtypeStruct(own.shape, kind) for own, kind in zip(owns, kinds)]
    return pl.pallas_call(join_body, out_shape=outs, compiler_params=SMALL)(came, *owns)


def total_body(plan, *refs):
    out = refs[-1]
    for walker, halves in enumerate(plan):

        @pl.when(pl.program_id(0) == walker)
        def add(halves=halves):
            rows = []
            for parts in halves:
                total = None
                for at, low, high in parts:
                    value = refs[at][low:high, :].astype(jnp.float32)
                    total = value if total is None else total + value
                rows.append(total)
            out[0] = -jnp.concatenate(rows, axis=0).T


def totals_of(values, plan):
    part, owned = values[0].shape
    return pl.pallas_call(
        functools.partial(total_body, plan),
        grid=(len(plan),),
        in_specs=[VMEM] * len(values),
        out_specs=pl.BlockSpec((1, owned, part * HALVES), lambda walker: (walker, 0, 0)),
        out_shape=jax.ShapeDtypeStruct((len(plan), owned, part * HALVES), jnp.float32),
        compiler_params=SMALL,
    )(*values)


def parts_of(stage, stages, vectors):
    if stage == 0:
        return [0, vectors // 4, vectors]
    if stage == stages - 1:
        return [0, vectors - vectors // 4, vectors]
    return [0, vectors]


def paired(shape, chol_half, theta):
    return in_order(shape, chol_half, theta)


def in_order(shape, chol_half, theta):
    shards = shape["vec"]
    vectors, width, _ = chol_half.shape
    walkers = theta.shape[0]
    position = lax.axis_index("vec")
    place = position.reshape(1)
    factors = []
    for half in range(HALVES):
        factors.append(loaded(place, chol_half, half))

    def flat(grp, vec, occ, wlk):
        return ((grp * shape["vec"] + vec) * shape["occ"] + occ) * shape["wlk"] + wlk

    def moved(value, hop, across=False):
        pairs = [
            (flat(grp, vec, occ, wlk), flat(grp, peer(vec, hop, shards), 1 - occ if across else occ, wlk))
            for grp in range(shape["grp"])
            for vec in range(shards)
            for occ in range(shape["occ"])
            for wlk in range(shape["wlk"])
        ]
        return lax.ppermute(value, AXES, pairs)

    hops = range(1, shards)
    near = [theta[0]] + [moved(theta[0], hop) for hop in hops]
    across = moved(theta, 0, True)
    blocks = [near + [across[0]] + [moved(near[hop], 0, True) for hop in hops]]
    for walker in range(1, walkers):
        both = jnp.concatenate([theta[walker], across[walker]], axis=1)
        pieces = {hop: moved(both, hop) for hop in hops if hop != passed_on(shards)}
        if passed_on(shards):
            pieces[passed_on(shards)] = moved(pieces[shards - 1], 1)
        blocks.append([both] + [pieces[hop] for hop in hops])

    stages = walkers * HALVES
    sides = []
    for stage in range(stages):
        owns, fars = [], []
        cuts = parts_of(stage, stages, vectors)
        for part in zip(cuts[:-1], cuts[1:]):
            own, far = amplitudes_of(place, factors[stage % HALVES], blocks[stage // HALVES], part, width, shards)
            owns.append(own)
            fars.append(moved(far, 0, True))
        sides.append((owns, fars))

    arrived = []
    for stage in range(stages - 1):
        got = gradients_of(place, factors, *sides[stage], shards)
        arrived.append([got[0]] + [moved(got[hop], hop) for hop in hops])
    *kept, crossing = split_sums(arrived)
    part = width // HALVES
    values = [*kept, moved(crossing, 0, True)]
    plan = [[(stage, 0, part), (len(kept), stage * part, (stage + 1) * part)] for stage in range(len(kept))]

    owns, fars = sides[-1]
    groups = groups_of(shards)
    (carried,) = gradients_of(place, factors, owns[:1], fars[:1], shards, more=True)
    cut = parts_of(stages - 1, stages, vectors)[1]
    ends = [None] * shards
    for group in groups:
        *own, far = gradients_of(place, factors, owns[1:], fars[1:], shards, cut, group, carried)
        came = moved(far, 0, True)
        joined = join_sums(came, own, [jnp.bfloat16 if hop else jnp.float32 for hop in group])
        for hop, value in zip(group, joined):
            ends[hop] = moved(value, hop) if hop else value
    plan.append([(len(values) + at, 0, part) for at in range(shards)])
    values += ends
    return totals_of(values, [plan[walker * HALVES : (walker + 1) * HALVES] for walker in range(walkers)])


def solution(mesh):
    placed = (P(("grp", "vec"), "occ", None), P(("grp", "wlk"), "vec", "occ"))
    pairs = mesh.shape["occ"] == 2
    return jax.shard_map(
        functools.partial(paired, dict(mesh.shape)) if pairs else general,
        mesh=mesh,
        in_specs=placed,
        out_specs=P(("grp", "wlk"), "vec", "occ"),
        check_vma=False,
    )
```

```python
import functools

import jax
import jax.numpy as jnp
from jax import lax
from jax.experimental import pallas as pl
from jax.experimental.pallas import tpu as pltpu
from jax.sharding import PartitionSpec as P


AXES = ("grp", "vec", "occ", "wlk")
HALVES = 2
STREAMS = 4
BLOCK = 8
LARGE = pltpu.CompilerParams(vmem_limit_bytes=44 * 2**20)
SMALL = pltpu.CompilerParams(vmem_limit_bytes=24 * 2**20)


def general(chol_half, theta):
    widened = lax.all_gather(theta, "occ", axis=2, tiled=True)
    amplitude_sums = jnp.einsum(
        "gip,wpj->wgij",
        chol_half,
        lax.all_gather(widened, "vec", axis=1, tiled=True),
        preferred_element_type=jnp.float32,
    )
    amplitudes = amplitude_sums.astype(jnp.bfloat16)
    swapped = lax.all_to_all(amplitudes, "occ", split_axis=3, concat_axis=2, tiled=True)
    summed_rows = lax.psum_scatter(
        jnp.einsum("gap,wgba->pwb", chol_half, swapped, preferred_element_type=jnp.float32),
        "vec",
        scatter_dimension=0,
        tiled=True,
    )
    owned = lax.psum_scatter(summed_rows, "occ", scatter_dimension=2, tiled=True)
    return -jnp.transpose(owned, (1, 0, 2))


VMEM = pl.BlockSpec(memory_space=pltpu.VMEM)
SMEM = pl.BlockSpec(memory_space=pltpu.SMEM)


def peer(position, hop, shards, back=False):
    if shards & (shards - 1) == 0:
        return position ^ hop
    moved = position + (shards - hop if back else hop)
    return moved % shards if isinstance(moved, int) else lax.rem(moved, shards)


def hops_of(shards):
    return sorted(range(1, shards), key=lambda hop: (hop != shards - 1, hop))


def passed_on(shards):
    return shards - 2 if shards > 2 and shards & (shards - 1) == 0 else None


def groups_of(shards):
    hops = list(range(shards - 1, -1, -1))
    return [hops[: shards // 2], hops[shards // 2 :]]


def by_neighbour(shards):
    return 1 if shards > 2 else None


def rows_of(hop, shards, owned):
    cut = owned // 2 if shards > 2 and hop == hops_of(shards)[-1] else owned
    return [(low, low + cut) for low in range(0, owned, cut)]


def load_body(half, place, source, out, arrived):
    del place
    vectors, part = out.shape[:2]
    cuts = [vectors * at // STREAMS for at in range(STREAMS + 1)]
    copies = []
    for at, (low, high) in enumerate(zip(cuts[:-1], cuts[1:])):
        some = pl.ds(low, high - low)
        copies.append(pltpu.make_async_copy(source.at[some, pl.ds(half * part, part)], out.at[some], arrived.at[at]))
    for copy in copies:
        copy.start()
    for copy in copies:
        copy.wait()


def loaded(place, factors, half):
    vectors, width, orbitals = factors.shape
    return pl.pallas_call(
        functools.partial(load_body, half),
        in_specs=[SMEM, pl.BlockSpec(memory_space=pltpu.HBM)],
        out_specs=VMEM,
        out_shape=pltpu.VMEM((vectors, width // HALVES, orbitals), factors.dtype),
        scratch_shapes=[pltpu.SemaphoreType.DMA((STREAMS,))],
        compiler_params=LARGE,
    )(place, factors)


def amplitude_body(shards, layout, low, high, place, factors, *refs):
    pieces, own, far, rows = refs[:-3], refs[-3], refs[-2], refs[-1]
    owned, width = rows.shape[0] // shards, own.shape[1]
    for piece, (hop, row, column) in zip(pieces, layout):
        at = pl.multiple_of(peer(place[0], hop, shards, True) * owned + row, piece.shape[0])
        rows[pl.ds(at, piece.shape[0]), column : column + piece.shape[1]] = piece[...]
    part = factors.shape[1]
    for first in range(low, high, BLOCK):
        taken = jnp.concatenate([factors[g] for g in range(first, min(first + BLOCK, high))], axis=0)
        sums = jnp.dot(taken, rows[...], preferred_element_type=jnp.float32).astype(jnp.bfloat16)
        at = (first - low) * part
        own[at : at + sums.shape[0], :] = sums[:, :width]
        far[at : at + sums.shape[0], :] = sums[:, width:]


def amplitudes_of(place, factors, pieces, vectors, width, shards):
    pieces, layout = [piece[0] for piece in pieces], tuple(piece[1:] for piece in pieces)
    orbitals = factors.shape[2]
    count = (vectors[1] - vectors[0]) * factors.shape[1]
    return pl.pallas_call(
        functools.partial(amplitude_body, shards, layout, *vectors),
        in_specs=[SMEM] + [VMEM] * (1 + len(pieces)),
        out_specs=[VMEM] * 2,
        scratch_shapes=[pltpu.VMEM((orbitals, 2 * width), jnp.bfloat16)],
        out_shape=[jax.ShapeDtypeStruct((count, width), jnp.bfloat16)] * 2,
        compiler_params=SMALL,
        cost_estimate=pl.CostEstimate(flops=4 * count * orbitals * width, transcendentals=0, bytes_accessed=2 * count * orbitals),
    )(place, factors, *pieces)


def gradient_body(shards, parts, first, carried, group, place, *refs):
    owns, fars, factors = refs[:parts], refs[parts : 2 * parts], refs[2 * parts : 2 * parts + HALVES]
    outs, sums = refs[2 * parts + HALVES + carried : -1], refs[-1]
    width = owns[0].shape[1]
    part = width // HALVES
    slots = [(at, g) for at, own in enumerate(owns) for g in range(own.shape[0] // part)]
    owned = factors[0].shape[2] // shards

    def wide(vectors):
        sides = [jnp.concatenate([side[at][g * part : (g + 1) * part, :] for at, g in vectors], axis=1) for side in (owns, fars)]
        return jnp.concatenate(sides, axis=0)

    def columns_of(hop):
        return pl.ds(pl.multiple_of(peer(place[0], hop, shards) * owned, owned), owned)

    if group is not None:
        taken = wide(slots)
        for at, hop in enumerate(group):
            columns = columns_of(hop)
            rows = jnp.concatenate([loaded[g, :, columns] for g in range(first, first + len(slots)) for loaded in factors], axis=0)
            total = refs[2 * parts + HALVES][:, columns] + jnp.dot(taken, rows, preferred_element_type=jnp.float32)
            outs[at][...] = total[:part]
            outs[-1][:, at * owned : (at + 1) * owned] = total[part:].astype(jnp.bfloat16)
        return

    for seen in range(0, len(slots), BLOCK):
        vectors = slots[seen : seen + BLOCK]
        low = first + seen
        rows = jnp.concatenate([loaded[g] for g in range(low, low + len(vectors)) for loaded in factors], axis=0)
        grown = jnp.dot(wide(vectors), rows, preferred_element_type=jnp.float32)
        if seen == 0:
            sums[...] = grown
        else:
            sums[...] += grown
    if len(outs) == 1:
        outs[0][...] = sums[...]
        return
    for hop in range(shards):
        outs[hop][...] = sums[:, columns_of(hop)].astype(outs[hop].dtype)


def gradients_of(place, factors, owns, fars, shards, first=0, group=None, carried=None, more=False):
    orbitals, width = factors[0].shape[2], owns[0].shape[1]
    part, owned = width // HALVES, orbitals // shards
    outs = [jax.ShapeDtypeStruct((2 * part, owned), jnp.bfloat16 if hop else jnp.float32) for hop in range(shards)]
    if more:
        outs = [jax.ShapeDtypeStruct((2 * part, orbitals), jnp.float32)]
    elif group:
        outs = [jax.ShapeDtypeStruct((part, owned), jnp.float32)] * len(group)
        outs += [jax.ShapeDtypeStruct((part, owned * len(group)), jnp.bfloat16)]
    count = sum(own.shape[0] for own in owns) * HALVES
    values = [place, *owns, *fars, *factors] + ([] if carried is None else [carried])
    return pl.pallas_call(
        functools.partial(gradient_body, shards, len(owns), first, 0 if carried is None else 1, group),
        in_specs=[SMEM] + [VMEM] * (len(values) - 1),
        out_specs=[VMEM] * len(outs),
        scratch_shapes=[pltpu.VMEM((2 * part, orbitals), jnp.float32)],
        out_shape=outs,
        compiler_params=SMALL,
        cost_estimate=pl.CostEstimate(flops=4 * count * orbitals * part, transcendentals=0, bytes_accessed=2 * count * orbitals),
    )(*values)


def split_body(each, *refs):
    inputs, outs = refs[: -(len(refs) // (each + 1)) - 1], refs[-(len(refs) // (each + 1)) - 1 :]
    for stage, own in enumerate(outs[:-1]):
        parts = inputs[stage * each : (stage + 1) * each]
        total = parts[0][...].astype(jnp.float32)
        for part in parts[1:]:
            total = total + part[...].astype(jnp.float32)
        half = own.shape[0]
        own[...] = total[:half]
        outs[-1][stage * half : (stage + 1) * half, :] = total[half:].astype(jnp.bfloat16)


def split_sums(stages):
    rows, columns = stages[0][0].shape
    outs = [jax.ShapeDtypeStruct((rows // 2, columns), jnp.float32)] * len(stages)
    outs += [jax.ShapeDtypeStruct((len(stages) * (rows // 2), columns), jnp.bfloat16)]
    flat = [part for stage in stages for part in stage]
    return pl.pallas_call(functools.partial(split_body, len(stages[0])), out_shape=outs, compiler_params=SMALL)(*flat)


def join_body(came, *refs):
    count = len(refs) // 2
    for at in range(count):
        own, out = refs[at], refs[count + at]
        columns = own.shape[1]
        out[...] = (own[...] + came[:, at * columns : (at + 1) * columns].astype(jnp.float32)).astype(out.dtype)


def join_sums(came, owns, kinds):
    outs = [jax.ShapeDtypeStruct(own.shape, kind) for own, kind in zip(owns, kinds)]
    return pl.pallas_call(join_body, out_shape=outs, compiler_params=SMALL)(came, *owns)


def total_body(plan, *refs):
    out = refs[-1]
    for walker, halves in enumerate(plan):

        @pl.when(pl.program_id(0) == walker)
        def add(halves=halves):
            rows = []
            for parts in halves:
                total = None
                for at, low, high in parts:
                    value = refs[at][low:high, :].astype(jnp.float32)
                    total = value if total is None else total + value
                rows.append(total)
            out[0] = -jnp.concatenate(rows, axis=0).T


def totals_of(values, plan):
    part, owned = values[0].shape
    return pl.pallas_call(
        functools.partial(total_body, plan),
        grid=(len(plan),),
        in_specs=[VMEM] * len(values),
        out_specs=pl.BlockSpec((1, owned, part * HALVES), lambda walker: (walker, 0, 0)),
        out_shape=jax.ShapeDtypeStruct((len(plan), owned, part * HALVES), jnp.float32),
        compiler_params=SMALL,
    )(*values)


def parts_of(stage, stages, vectors):
    if stage == 0:
        return [0, vectors // 4, vectors]
    if stage == stages - 1:
        return [0, vectors - vectors // 4, vectors]
    return [0, vectors]


def paired(shape, chol_half, theta):
    return in_order(shape, chol_half, theta)


def in_order(shape, chol_half, theta):
    shards = shape["vec"]
    vectors, width, _ = chol_half.shape
    walkers = theta.shape[0]
    position = lax.axis_index("vec")
    place = position.reshape(1)
    factors = []
    for half in range(HALVES):
        factors.append(loaded(place, chol_half, half))

    def flat(grp, vec, occ, wlk):
        return ((grp * shape["vec"] + vec) * shape["occ"] + occ) * shape["wlk"] + wlk

    def moved(value, hop, across=False):
        pairs = [
            (flat(grp, vec, occ, wlk), flat(grp, peer(vec, hop, shards), 1 - occ if across else occ, wlk))
            for grp in range(shape["grp"])
            for vec in range(shards)
            for occ in range(shape["occ"])
            for wlk in range(shape["wlk"])
        ]
        return lax.ppermute(value, AXES, pairs)

    hops = range(1, shards)
    across = moved(theta, 0, True)
    block = [(theta[0], 0, 0, 0), (across[0], 0, 0, width)]
    for hop in hops:
        for low, high in rows_of(hop, shards, theta.shape[1]):
            came = moved(theta[0, low:high], hop)
            block.append((came, hop, low, 0))
            if hop != by_neighbour(shards):
                block.append((moved(came, 0, True), hop, low, width))
    if by_neighbour(shards):
        block.append((moved(across[0], by_neighbour(shards)), by_neighbour(shards), 0, width))
    blocks = [block]
    for walker in range(1, walkers):
        both = jnp.concatenate([theta[walker], across[walker]], axis=1)
        pieces = {hop: moved(both, hop) for hop in hops if hop != passed_on(shards)}
        if passed_on(shards):
            pieces[passed_on(shards)] = moved(pieces[shards - 1], 1)
        blocks.append([(both, 0, 0, 0)] + [(pieces[hop], hop, 0, 0) for hop in hops])

    stages = walkers * HALVES
    sides = []
    for stage in range(stages):
        owns, fars = [], []
        cuts = parts_of(stage, stages, vectors)
        for part in zip(cuts[:-1], cuts[1:]):
            own, far = amplitudes_of(place, factors[stage % HALVES], blocks[stage // HALVES], part, width, shards)
            owns.append(own)
            fars.append(moved(far, 0, True))
        sides.append((owns, fars))

    arrived = []
    for stage in range(stages - 1):
        got = gradients_of(place, factors, *sides[stage], shards)
        arrived.append([got[0]] + [moved(got[hop], hop) for hop in hops])
    *kept, crossing = split_sums(arrived)
    part = width // HALVES
    values = [*kept, moved(crossing, 0, True)]
    plan = [[(stage, 0, part), (len(kept), stage * part, (stage + 1) * part)] for stage in range(len(kept))]

    owns, fars = sides[-1]
    groups = groups_of(shards)
    (carried,) = gradients_of(place, factors, owns[:1], fars[:1], shards, more=True)
    cut = parts_of(stages - 1, stages, vectors)[1]
    ends = [None] * shards
    for group in groups:
        *own, far = gradients_of(place, factors, owns[1:], fars[1:], shards, cut, group, carried)
        came = moved(far, 0, True)
        joined = join_sums(came, own, [jnp.bfloat16 if hop else jnp.float32 for hop in group])
        for hop, value in zip(group, joined):
            ends[hop] = moved(value, hop) if hop else value
    plan.append([(len(values) + at, 0, part) for at in range(shards)])
    values += ends
    return totals_of(values, [plan[walker * HALVES : (walker + 1) * HALVES] for walker in range(walkers)])


def solution(mesh):
    placed = (P(("grp", "vec"), "occ", None), P(("grp", "wlk"), "vec", "occ"))
    pairs = mesh.shape["occ"] == 2
    return jax.shard_map(
        functools.partial(paired, dict(mesh.shape)) if pairs else general,
        mesh=mesh,
        in_specs=placed,
        out_specs=P(("grp", "wlk"), "vec", "occ"),
        check_vma=False,
    )
```
